512 devices in a mesh: wide: 64 (over y, z_lo, x), narrow: 8 (over z_hi, core).
Axes of the slice: x: 4, y: 8, z: 8 (z_hi: 4, z_lo: 2; z = z_hi * 2 + z_lo), core: 2. Of those that a mesh axis runs over, the one named last changes fastest.
Arguments:
- conc: float32 [2, 128, 64, 1024], P(None, 'wide', 'narrow'), may hold values from 0.2 to 2
- potential: float32 [128, 64, 1024], P('wide', 'narrow'), may hold values from -6 to 6
- velocity: float32 [3, 128, 64, 1024], P(None, 'wide', 'narrow'), may hold values from -3 to 3
- solid: int32 [128, 64, 1024], P('wide', 'narrow'), may hold values 0 or 1
- fixed_charge: float32 [128, 64, 1024], P('wide', 'narrow'), may hold values from -6 to 6
Outputs:
- new_conc: float32 [2, 128, 64, 1024], P(None, 'wide', 'narrow')
- new_potential: float32 [128, 64, 1024], P('wide', 'narrow')
The draws below stay inside these ranges and needn't reach their ends.
All inputs are finite; a program needn't handle non-finite values. No bound on the sum of `solid` on one device may be relied on, other than what follows from the above.
Results may differ from the reference program's by a relative error of at most 0.0001.
Values sent between devices are 32-bit elements; how exact they have to be, the bound alone decides.
A program may use at most 64 MiB of HBM per device.

```python
import math
import jax
import jax.numpy as jnp
from jax import lax

NZ = 1024
NX = 128
NY = 64


def with_ends(values, key, smallest, top_value):
    extent = values.shape
    index_at = [jax.random.randint(jax.random.fold_in(key, axis), (), 0, extent[axis]) for axis in range(len(extent))]
    values = values.at[tuple(index_at)].set(smallest)
    longest = extent.index(max(extent))
    index_at[longest] = (index_at[longest] + 1) % extent[longest]
    return values.at[tuple(index_at)].set(top_value)


def shard_levels(rng, extent, pieces, least, high):
    gain = 1.0
    for position, blocks in pieces:
        heights = jax.random.uniform(jax.random.fold_in(jax.random.fold_in(rng, 6), position), (blocks,), jnp.float32, least / len(pieces), high / len(pieces))
        gain = gain * jnp.repeat(jnp.exp(heights), extent[position] // blocks).reshape((-1,) + (1,) * (len(extent) - 1 - position))
    return gain


def scatter_about(own_key, dims, width, most, split=(), kind=jnp.bfloat16):
    values = width * jax.random.normal(own_key, dims, jnp.float32)
    if split:
        values = values * shard_levels(own_key, dims, split, -0.22, 0.18)
    return jnp.clip(values, -most, most).astype(kind)


def setup_inputs(seed: int = 0) -> dict:
    keys = jax.random.split(jax.random.key(seed), 6)
    return {
        "conc": jnp.clip(jnp.exp(math.log(2.0) - 2.3025851 * jax.random.uniform(keys[0], (2, NX, NY, NZ), jnp.float32) ** shard_levels(keys[0], (2, NX, NY, NZ), ((1, 64), (2, 8)), -0.2, 0.2)), 0.2, 2.0),
        "potential": scatter_about(keys[1], (NX, NY, NZ), 1.0, 6.0, ((0, 64), (1, 8)), jnp.float32),
        "velocity": scatter_about(keys[2], (3, NX, NY, NZ), 0.5, 3.0, ((1, 64), (2, 8)), jnp.float32),
        "solid": with_ends((jax.random.randint(keys[3], (NX, NY, NZ), 0, 5) < 1).astype(jnp.int32), jax.random.fold_in(keys[3], 1), 0, 1),
        "fixed_charge": scatter_about(keys[4], (NX, NY, NZ), 1.0, 6.0, ((0, 64), (1, 8)), jnp.float32),
    }


def inner_part(array, axis, margin):
    return lax.slice_in_dim(array, margin, array.shape[axis] - margin, axis=axis)

def explicit_rhs(padded, fixed_charge):
    mobility = jnp.array([0.25, -0.25], jnp.float32).reshape(2, 1, 1, 1)
    total = None
    for direction in (1, 2, 3):
        sub = padded
        for other in (1, 2, 3):
            if other != direction:
                sub = inner_part(sub, other, 2)
        field = sub[2]
        length = field.shape[direction - 1]
        grad = (lax.slice_in_dim(field, 2, length, axis=direction - 1) - lax.slice_in_dim(field, 0, length - 2, axis=direction - 1)) * 0.5
        inner = inner_part(sub, direction, 1)
        flux = inner[6][None] * inner[0:2] * (inner[2 + direction][None] - mobility * grad[None])
        size = flux.shape[direction]
        diverge = (lax.slice_in_dim(flux, 2, size, axis=direction) - lax.slice_in_dim(flux, 0, size - 2, axis=direction)) * 0.5
        total = diverge if total is None else total + diverge
    core = padded
    for axis in (1, 2, 3):
        core = inner_part(core, axis, 2)
    fluid = core[6]
    rhs_conc = fluid[None] * (core[0:2] - 0.5 * total)
    charge = fluid * (core[0] - core[1]) + (1.0 - fluid) * fixed_charge
    rhs_field = core[2] + 2.0 * charge
    return jnp.concatenate([rhs_conc, rhs_field[None], fluid[None]], 0)

def solve_lines(block, axis):
    fields = jnp.moveaxis(block[:3], axis, -1)
    fluid = jnp.moveaxis(block[3], axis - 1, -1)
    masks = jnp.stack([fluid, fluid, jnp.ones_like(fluid)])
    shape_one = (3,) + (1,) * (masks.ndim - 1)
    rates = jnp.array([8.0, 5.0, 16.0], jnp.float32).reshape(shape_one)
    outer = jnp.array([0.0, 0.0, 1.0], jnp.float32).reshape(shape_one) * jnp.ones_like(masks[..., :1])
    nothing = jnp.zeros_like(masks[..., :1])
    prev_in = jnp.concatenate([nothing, masks[..., :-1]], -1)
    next_in = jnp.concatenate([masks[..., 1:], nothing], -1)
    prev_out = jnp.concatenate([outer, masks[..., :-1]], -1)
    next_out = jnp.concatenate([masks[..., 1:], outer], -1)
    diag = 1.0 + rates * masks * (prev_out + next_out)
    lower = -rates * masks * prev_in
    upper = -rates * masks * next_in
    solved = lax.linalg.tridiagonal_solve(lower, diag, upper, fields[..., None])[..., 0]
    return jnp.moveaxis(solved, -1, axis)

def reference(conc, potential, velocity, solid, fixed_charge):
    fluid = (1 - solid).astype(jnp.float32)
    stacked = jnp.concatenate([conc, potential[None], velocity, fluid[None]], 0)
    padded = jnp.pad(stacked, ((0, 0), (2, 2), (2, 2), (2, 2)))
    rhs = explicit_rhs(padded, fixed_charge)
    after_x = jnp.concatenate([solve_lines(rhs, 1), rhs[3:]], 0)
    after_y = jnp.concatenate([solve_lines(after_x, 2), rhs[3:]], 0)
    result = solve_lines(after_y, 3)
    return (result[:2], result[2])
```

```python
import jax
import jax.numpy as jnp
from jax import lax
from jax.experimental import pallas as pl
from jax.experimental.pallas import tpu as pltpu
from jax.sharding import PartitionSpec as P

F32 = jnp.float32
MESH = pl.DeviceIdType.MESH
LANES = 128
ROWS = 8
CHUNK = 8


def pcr(here, prev, succ):
    a, c, d = here
    ap, cp, dp = prev
    an, cn, dn = succ
    r = 1.0 / (1.0 - a * cp - c * an)
    return -(a * ap) * r, -(c * cn) * r, (d - a * dp - c * dn) * r


def row_facts():
    row = lax.broadcasted_iota(jnp.int32, (1, ROWS, LANES), 1)
    even = row % 2 == 0
    is_pot = row >= 4
    rate = jnp.where(row < 2, 8.0, jnp.where(row < 4, 5.0, jnp.where(row < 6, 16.0, 0.0)))
    return even, is_pot, rate.astype(F32)


def masks(tiles):
    return tiles[:, 6:7, :], tiles[:, 7:8, :]


def normal_bands(tiles, mask, mask_prev, mask_next, rate, is_first, is_last):
    rm = rate * mask
    inv = 1.0 / (1.0 + rm * (mask_prev + mask_next))
    lower = jnp.where(is_first, 0.0, -rm * mask_prev * inv)
    upper = jnp.where(is_last, 0.0, -rm * mask_next * inv)
    return lower, upper, tiles * inv


def solve_tiles(src_ref, src_pad, bufs, dst_ref, dst_pad, count, pad, paired):
    def build(i, _):
        even, is_pot, rate = row_facts()
        base = src_pad + i * CHUNK
        tiles = src_ref[pl.ds(base, CHUNK)]
        m0, m1 = masks(tiles)
        p0, p1 = masks(src_ref[pl.ds(base - 1, CHUNK)])
        n0, n1 = masks(src_ref[pl.ds(base + 1, CHUNK)])
        own = jnp.where(is_pot, 1.0, jnp.where(even, m0, m1))
        place = i * CHUNK + lax.broadcasted_iota(jnp.int32, (CHUNK, ROWS, LANES), 0)
        first = place == 0
        last = place == count - 1
        if paired:
            before = jnp.where(is_pot, 1.0, jnp.where(even, p1, m0))
            after = jnp.where(is_pot, 1.0, jnp.where(even, m1, n0))
            first = first & even
            last = last & jnp.logical_not(even)
        else:
            before = jnp.where(is_pot, 1.0, jnp.where(even, p0, p1))
            after = jnp.where(is_pot, 1.0, jnp.where(even, n0, n1))
        bands = normal_bands(tiles, own, before, after, rate, first, last)
        for k in range(3):
            bufs[0][k, pl.ds(pad + i * CHUNK, CHUNK)] = bands[k]
        return 0

    lax.fori_loop(0, count // CHUNK, build, 0)
    now = 0

    def window(buf, base):
        return tuple(buf[k, pl.ds(base, CHUNK)] for k in range(3))

    if paired:

        def pair_step(i, _):
            even, _, _ = row_facts()
            base = pad + i * CHUNK
            here = window(bufs[0], base)
            left = window(bufs[0], base - 1)
            right = window(bufs[0], base + 1)

            def up(v):
                return pltpu.roll(v, ROWS - 1, 1)

            def down(v):
                return pltpu.roll(v, 1, 1)

            prev = tuple(jnp.where(even, up(l), down(h)) for l, h in zip(left, here))
            succ = tuple(jnp.where(even, up(h), down(r)) for h, r in zip(here, right))
            for k, v in enumerate(pcr(here, prev, succ)):
                bufs[1][k, pl.ds(base, CHUNK)] = v
            return 0

        lax.fori_loop(0, count // CHUNK, pair_step, 0)
        now = 1

    spacing = 1
    while spacing < count:
        source, target = bufs[now], bufs[1 - now]
        final = spacing * 2 >= count

        def step(i, _, source=source, target=target, spacing=spacing, final=final):
            base = pad + i * CHUNK
            new = pcr(
                window(source, base), window(source, base - spacing), window(source, base + spacing)
            )
            if final:
                dst_ref[pl.ds(dst_pad + i * CHUNK, CHUNK)] = new[2]
            else:
                for k in range(3):
                    target[k, pl.ds(base, CHUNK)] = new[k]
            return 0

        lax.fori_loop(0, count // CHUNK, step, 0)
        now = 1 - now
        spacing *= 2


def main_kernel(
    nw, nn, conc, pot, vel, solid, fixed, out,
    sx_r, sx_l, rx_l, rx_r, sy_u, sy_d, ry_d, ry_u, packed, stage, xr, xsol, xback,
    yr, ysol, buf_a, buf_b,
    hs, hr, xs_s, xs_r, xb_s, xb_r, ys_s, ys_r, yb_s, yb_r,
):
    wide = lax.axis_index("wide")
    narrow = lax.axis_index("narrow")
    right = lax.rem(wide + 1, nw)
    left = lax.rem(wide + nw - 1, nw)
    upper = lax.rem(narrow + 1, nn)
    lower = lax.rem(narrow + nn - 1, nn)
    zt = pot.shape[2] // LANES
    pad = (buf_a.shape[1] - nw) // 2

    barrier = pltpu.get_barrier_semaphore()

    def greet_wide(k, _):
        pl.semaphore_signal(
            barrier, inc=1, device_id={"wide": lax.rem(wide + k, nw)}, device_id_type=MESH
        )
        return 0

    def greet_narrow(k, _):
        pl.semaphore_signal(
            barrier, inc=1, device_id={"narrow": lax.rem(narrow + k, nn)}, device_id_type=MESH
        )
        return 0

    lax.fori_loop(1, nw, greet_wide, 0)
    lax.fori_loop(1, nn, greet_narrow, 0)

    fl = [(1 - solid[x]).astype(F32) for x in range(2)]
    act = [[fl[x] * conc[k, x] for x in range(2)] for k in range(2)]
    for k in range(2):
        sx_r[k] = act[k][1]
        sx_l[k] = act[k][0]
    sx_r[2] = vel[0, 1]
    sx_l[2] = vel[0, 0]
    for x in range(2):
        sx_r[3 + x] = pot[x]
        sx_l[3 + x] = pot[x]
        for k in range(2):
            sy_u[x, k : k + 1] = act[k][x][7:8]
            sy_d[x, k : k + 1] = act[k][x][0:1]
        sy_u[x, 2:3] = vel[1, x, 7:8]
        sy_d[x, 2:3] = vel[1, x, 0:1]
        sy_u[x, 3:5] = pot[x, 6:8]
        sy_d[x, 3:5] = pot[x, 0:2]
        sy_u[x, 5:8] = jnp.zeros((3, pot.shape[2]), F32)
        sy_d[x, 5:8] = jnp.zeros((3, pot.shape[2]), F32)
    nothing = jnp.zeros((pad, ROWS, LANES), F32)
    for buf in (buf_a, buf_b):
        for k in range(3):
            buf[k, pl.ds(0, pad)] = nothing
            buf[k, pl.ds(pad + nw, pad)] = nothing
    for ref in (xr, yr):
        ref[pl.ds(0, 1)] = nothing[:1]
        ref[pl.ds(nw + 1, 1)] = nothing[:1]

    pl.semaphore_wait(barrier, nw + nn - 2)

    halos = [
        pltpu.make_async_remote_copy(
            src_ref=src, dst_ref=dst, send_sem=hs.at[n], recv_sem=hr.at[n],
            device_id=peer, device_id_type=MESH,
        )
        for n, (src, dst, peer) in enumerate(
            (
                (sx_r, rx_l, {"wide": right}),
                (sx_l, rx_r, {"wide": left}),
                (sy_u, ry_d, {"narrow": upper}),
                (sy_d, ry_u, {"narrow": lower}),
            )
        )
    ]
    for copy in halos:
        copy.start()

    shape = (ROWS, pot.shape[2])
    lane = lax.broadcasted_iota(jnp.int32, shape, 1)
    sub = lax.broadcasted_iota(jnp.int32, shape, 0)
    length = pot.shape[2]

    def z_next(v):
        return jnp.where(lane == length - 1, 0.0, pltpu.roll(v, length - 1, 1))

    def z_prev(v):
        return jnp.where(lane == 0, 0.0, pltpu.roll(v, 1, 1))

    def y_next(v, edge):
        return jnp.where(sub == ROWS - 1, edge, pltpu.roll(v, ROWS - 1, 0))

    def y_prev(v, edge):
        return jnp.where(sub == 0, edge, pltpu.roll(v, 1, 0))

    tilt = (0.125, -0.125)
    div_z = []
    for x in range(2):
        p = pot[x]
        slope = z_next(p) - z_prev(p)
        row = []
        for k in range(2):
            q = act[k][x] * (vel[2, x] - tilt[k] * slope)
            row.append((z_next(q) - z_prev(q)) * 0.5)
        div_z.append(row)

    for copy in halos:
        copy.wait()

    has_left = wide > 0
    has_right = wide < nw - 1
    has_down = narrow > 0
    has_up = narrow < nn - 1

    def kept(flag, v):
        return jnp.where(flag, v, 0.0)

    def pack(row, v):
        for t in range(zt):
            packed[pl.ds((t * ROWS + row) * ROWS, ROWS), :] = v[:, t * LANES : (t + 1) * LANES]

    pots = [
        kept(has_left, rx_l[3]), kept(has_left, rx_l[4]), pot[0], pot[1],
        kept(has_right, rx_r[3]), kept(has_right, rx_r[4]),
    ]
    velx = [rx_l[2], vel[0, 0], vel[0, 1], rx_r[2]]
    for x in range(2):
        fixed_x = fixed[x]
        p = pot[x]
        down = kept(has_down, ry_d[x])
        up = kept(has_up, ry_u[x])
        slope_y = y_next(p, up[3:4]) - y_prev(p, down[4:5])
        slope_d = p[0:1] - down[3:4]
        slope_u = up[4:5] - p[7:8]
        for k in range(2):
            acts = [kept(has_left, rx_l[k]), act[k][0], act[k][1], kept(has_right, rx_r[k])]

            def flux_x(n):
                return acts[n] * (velx[n] - tilt[k] * (pots[n + 2] - pots[n]))

            div_x = (flux_x(x + 2) - flux_x(x)) * 0.5
            qy = act[k][x] * (vel[1, x] - tilt[k] * slope_y)
            q_down = down[k : k + 1] * (down[2:3] - tilt[k] * slope_d)
            q_up = up[k : k + 1] * (up[2:3] - tilt[k] * slope_u)
            div_y = (y_next(qy, q_up) - y_prev(qy, q_down)) * 0.5
            total = div_x + div_y + div_z[x][k]
            pack(2 * k + x, fl[x] * (conc[k, x] - 0.5 * total))
        charge = fl[x] * (conc[0, x] - conc[1, x]) + (1.0 - fl[x]) * fixed_x
        pack(4 + x, p + 2.0 * charge)
        pack(6 + x, fl[x])

    for t in range(zt):
        for y in range(ROWS):
            stage[t * ROWS + y] = packed[pl.ds(t * ROWS * ROWS + y, ROWS, stride=ROWS), :]

    def x_copy(k):
        peer = lax.rem(wide + k, nw)
        return pltpu.make_async_remote_copy(
            src_ref=stage.at[peer], dst_ref=xr.at[wide + 1],
            send_sem=xs_s.at[peer], recv_sem=xs_r.at[wide],
            device_id={"wide": peer}, device_id_type=MESH,
        )

    def x_arrival(k):
        peer = lax.rem(wide + k, nw)
        return pltpu.make_async_remote_copy(
            src_ref=stage.at[peer], dst_ref=xr.at[peer + 1],
            send_sem=xs_s.at[peer], recv_sem=xs_r.at[peer],
            device_id={"wide": peer}, device_id_type=MESH,
        )

    def back_copy(k):
        peer = lax.rem(wide + k, nw)
        return pltpu.make_async_remote_copy(
            src_ref=xsol.at[peer], dst_ref=xback.at[wide],
            send_sem=xb_s.at[peer], recv_sem=xb_r.at[wide],
            device_id={"wide": peer}, device_id_type=MESH,
        )

    def back_arrival(k):
        peer = lax.rem(wide + k, nw)
        return pltpu.make_async_remote_copy(
            src_ref=xsol.at[peer], dst_ref=xback.at[peer],
            send_sem=xb_s.at[peer], recv_sem=xb_r.at[peer],
            device_id={"wide": peer}, device_id_type=MESH,
        )

    def group(index):
        return pl.ds(pl.multiple_of(index * ROWS, ROWS), ROWS)

    def y_copy(k):
        peer = lax.rem(narrow + k, nn)
        return pltpu.make_async_remote_copy(
            src_ref=xback.at[group(peer)], dst_ref=yr.at[pl.ds(narrow * ROWS + 1, ROWS)],
            send_sem=ys_s.at[peer], recv_sem=ys_r.at[narrow],
            device_id={"narrow": peer}, device_id_type=MESH,
        )

    def y_arrival(k):
        peer = lax.rem(narrow + k, nn)
        return pltpu.make_async_remote_copy(
            src_ref=xback.at[group(peer)], dst_ref=yr.at[pl.ds(peer * ROWS + 1, ROWS)],
            send_sem=ys_s.at[peer], recv_sem=ys_r.at[peer],
            device_id={"narrow": peer}, device_id_type=MESH,
        )

    def out_copy(k):
        peer = lax.rem(narrow + k, nn)
        return pltpu.make_async_remote_copy(
            src_ref=ysol.at[group(peer)], dst_ref=out.at[group(narrow)],
            send_sem=yb_s.at[peer], recv_sem=yb_r.at[narrow],
            device_id={"narrow": peer}, device_id_type=MESH,
        )

    def out_arrival(k):
        peer = lax.rem(narrow + k, nn)
        return pltpu.make_async_remote_copy(
            src_ref=ysol.at[group(peer)], dst_ref=out.at[group(peer)],
            send_sem=yb_s.at[peer], recv_sem=yb_r.at[peer],
            device_id={"narrow": peer}, device_id_type=MESH,
        )

    def start(copy_of, count):
        def body(k, _):
            copy_of(k).start()
            return 0

        lax.fori_loop(1, count, body, 0)

    def arrive(copy_of, count):
        def body(k, _):
            copy_of(k).wait_recv()
            return 0

        lax.fori_loop(1, count, body, 0)

    def drain(copy_of, count):
        def body(k, _):
            copy_of(k).wait_send()
            return 0

        lax.fori_loop(1, count, body, 0)

    bufs = (buf_a, buf_b)
    start(x_copy, nw)
    xr[pl.ds(wide + 1, 1)] = stage[pl.ds(wide, 1)]
    arrive(x_arrival, nw)
    solve_tiles(xr, 1, bufs, xsol, 0, nw, pad, True)
    start(back_copy, nw)
    xback[pl.ds(wide, 1)] = xsol[pl.ds(wide, 1)]
    arrive(back_arrival, nw)
    start(y_copy, nn)
    yr[pl.ds(narrow * ROWS + 1, ROWS)] = xback[group(narrow)]
    arrive(y_arrival, nn)
    solve_tiles(yr, 1, bufs, ysol, 0, nn * ROWS, pad, False)
    start(out_copy, nn)
    out[group(narrow)] = ysol[group(narrow)]
    arrive(out_arrival, nn)
    drain(x_copy, nw)
    drain(back_copy, nw)
    drain(y_copy, nn)
    drain(out_copy, nn)


def z_kernel(tiles, solid, new_conc, new_pot):
    length = solid.shape[2]
    shape = (ROWS, length)
    lane = lax.broadcasted_iota(jnp.int32, shape, 1)
    first = lane == 0
    last = lane == length - 1

    def source(row):
        return jnp.concatenate(
            [
                tiles[pl.ds(t * ROWS * ROWS + row, ROWS, stride=ROWS), :]
                for t in range(length // LANES)
            ],
            axis=1,
        )

    def solve(lower, upper, sources):
        spacing = 1
        while spacing < length:
            lower_prev, upper_prev = (pltpu.roll(v, spacing, 1) for v in (lower, upper))
            lower_next, upper_next = (pltpu.roll(v, length - spacing, 1) for v in (lower, upper))
            r = 1.0 / (1.0 - lower * upper_prev - upper * lower_next)
            sources = [
                (d - lower * pltpu.roll(d, spacing, 1) - upper * pltpu.roll(d, length - spacing, 1)) * r
                for d in sources
            ]
            lower, upper = -(lower * lower_prev) * r, -(upper * upper_next) * r
            spacing *= 2
        return sources

    for x in range(2):
        mask = (1 - solid[x]).astype(F32)
        before = jnp.where(first, 0.0, pltpu.roll(mask, 1, 1))
        after = jnp.where(last, 0.0, pltpu.roll(mask, length - 1, 1))
        for k, rate in enumerate((8.0, 5.0)):
            rm = rate * mask
            inv = 1.0 / (1.0 + rm * (before + after))
            (result,) = solve(
                -rm * before * inv, -rm * after * inv, [source(2 * k + x) * inv]
            )
            new_conc[k, x] = result
    inv = 1.0 / 33.0
    results = solve(
        jnp.where(first, 0.0, -16.0 * inv) * jnp.ones(shape, F32),
        jnp.where(last, 0.0, -16.0 * inv) * jnp.ones(shape, F32),
        [source(4) / 33.0, source(5) / 33.0],
    )
    for x in range(2):
        new_pot[x] = results[x]


def solution(mesh):
    nw, nn = mesh.shape["wide"], mesh.shape["narrow"]

    def shards(conc, potential, velocity, solid, fixed_charge):
        height = potential.shape[2]
        vmem = pl.BlockSpec(memory_space=pltpu.VMEM)
        tiles = (nw, ROWS, LANES)
        padded = (nw + 2, ROWS, LANES)
        plane = (5, ROWS, height)
        edge = (2, ROWS, height)
        bands = (3, 2 * nw, ROWS, LANES)
        dma = pltpu.SemaphoreType.DMA

        def body(*refs):
            main_kernel(nw, nn, *refs)

        after_y = pl.pallas_call(
            body,
            name="halo_x_y",
            out_shape=jax.ShapeDtypeStruct(tiles, F32),
            in_specs=[vmem] * 5,
            out_specs=vmem,
            scratch_shapes=[pltpu.VMEM(plane, F32)] * 4
            + [pltpu.VMEM(edge, F32)] * 4
            + [pltpu.VMEM((nw * ROWS, LANES), F32)]
            + [pltpu.VMEM(s, F32) for s in (tiles, padded, tiles, tiles, padded, tiles, bands, bands)]
            + [dma((4,)), dma((4,)), dma((nw,)), dma((nw,)), dma((nw,)), dma((nw,))]
            + [dma((nn,)), dma((nn,)), dma((nn,)), dma((nn,))],
            compiler_params=pltpu.CompilerParams(collective_id=0, has_side_effects=True),
        )(conc, potential, velocity, solid, fixed_charge)
        return pl.pallas_call(
            z_kernel,
            name="solve_z",
            out_shape=(
                jax.ShapeDtypeStruct(conc.shape, F32),
                jax.ShapeDtypeStruct(potential.shape, F32),
            ),
            in_specs=[vmem] * 2,
            out_specs=(vmem, vmem),
        )(after_y.reshape(nw * ROWS, LANES), solid)

    return jax.shard_map(
        shards,
        mesh=mesh,
        in_specs=(
            P(None, "wide", "narrow", None),
            P("wide", "narrow", None),
            P(None, "wide", "narrow", None),
            P("wide", "narrow", None),
            P("wide", "narrow", None),
        ),
        out_specs=(P(None, "wide", "narrow", None), P("wide", "narrow", None)),
        check_vma=False,
    )
```

```python
import jax
import jax.numpy as jnp
from jax import lax
from jax.experimental import pallas as pl
from jax.experimental.pallas import tpu as pltpu
from jax.sharding import PartitionSpec as P

F32 = jnp.float32
MESH = pl.DeviceIdType.MESH
LANES = 128
ROWS = 8
CHUNK = 8


def pcr(here, prev, succ):
    a, c, d = here
    ap, cp, dp = prev
    an, cn, dn = succ
    r = 1.0 / (1.0 - a * cp - c * an)
    return -(a * ap) * r, -(c * cn) * r, (d - a * dp - c * dn) * r


def row_facts():
    row = lax.broadcasted_iota(jnp.int32, (1, ROWS, LANES), 1)
    even = row % 2 == 0
    is_pot = row >= 4
    rate = jnp.where(row < 2, 8.0, jnp.where(row < 4, 5.0, jnp.where(row < 6, 16.0, 0.0)))
    return even, is_pot, rate.astype(F32)


def masks(tiles):
    return tiles[:, 6:7, :], tiles[:, 7:8, :]


def normal_bands(tiles, mask, mask_prev, mask_next, rate, is_first, is_last):
    rm = rate * mask
    inv = 1.0 / (1.0 + rm * (mask_prev + mask_next))
    lower = jnp.where(is_first, 0.0, -rm * mask_prev * inv)
    upper = jnp.where(is_last, 0.0, -rm * mask_next * inv)
    return lower, upper, tiles * inv


def solve_tiles(src_ref, src_pad, bufs, dst_ref, dst_pad, count, pad, paired):
    def build(i, _):
        even, is_pot, rate = row_facts()
        base = src_pad + i * CHUNK
        tiles = src_ref[pl.ds(base, CHUNK)]
        m0, m1 = masks(tiles)
        p0, p1 = masks(src_ref[pl.ds(base - 1, CHUNK)])
        n0, n1 = masks(src_ref[pl.ds(base + 1, CHUNK)])
        own = jnp.where(is_pot, 1.0, jnp.where(even, m0, m1))
        place = i * CHUNK + lax.broadcasted_iota(jnp.int32, (CHUNK, ROWS, LANES), 0)
        first = place == 0
        last = place == count - 1
        if paired:
            before = jnp.where(is_pot, 1.0, jnp.where(even, p1, m0))
            after = jnp.where(is_pot, 1.0, jnp.where(even, m1, n0))
            first = first & even
            last = last & jnp.logical_not(even)
        else:
            before = jnp.where(is_pot, 1.0, jnp.where(even, p0, p1))
            after = jnp.where(is_pot, 1.0, jnp.where(even, n0, n1))
        bands = normal_bands(tiles, own, before, after, rate, first, last)
        for k in range(3):
            bufs[0][k, pl.ds(pad + i * CHUNK, CHUNK)] = bands[k]
        return 0

    lax.fori_loop(0, count // CHUNK, build, 0)
    now = 0

    def window(buf, base):
        return tuple(buf[k, pl.ds(base, CHUNK)] for k in range(3))

    if paired:

        def pair_step(i, _):
            even, _, _ = row_facts()
            base = pad + i * CHUNK
            here = window(bufs[0], base)
            left = window(bufs[0], base - 1)
            right = window(bufs[0], base + 1)

            def up(v):
                return pltpu.roll(v, ROWS - 1, 1)

            def down(v):
                return pltpu.roll(v, 1, 1)

            prev = tuple(jnp.where(even, up(l), down(h)) for l, h in zip(left, here))
            succ = tuple(jnp.where(even, up(h), down(r)) for h, r in zip(here, right))
            for k, v in enumerate(pcr(here, prev, succ)):
                bufs[1][k, pl.ds(base, CHUNK)] = v
            return 0

        lax.fori_loop(0, count // CHUNK, pair_step, 0)
        now = 1

    spacing = 1
    while spacing < count:
        source, target = bufs[now], bufs[1 - now]
        final = spacing * 2 >= count

        def step(i, _, source=source, target=target, spacing=spacing, final=final):
            base = pad + i * CHUNK
            new = pcr(
                window(source, base), window(source, base - spacing), window(source, base + spacing)
            )
            if final:
                dst_ref[pl.ds(dst_pad + i * CHUNK, CHUNK)] = new[2]
            else:
                for k in range(3):
                    target[k, pl.ds(base, CHUNK)] = new[k]
            return 0

        lax.fori_loop(0, count // CHUNK, step, 0)
        now = 1 - now
        spacing *= 2


def main_kernel(
    nw, nn, conc, pot, vel, solid, fixed, out,
    sx_r, sx_l, rx_l, rx_r, sy_u, sy_d, ry_d, ry_u, packed, stage, xr, xsol, xback,
    buf_a, buf_b, y_am, y_m, y_c, y_left, y_right, y_sol,
    edge_s, edge_r, dat_s, dat_r, ends_s, ends_r, ring,
    hs, hr, xe_s, xe_r, xs_s, xs_r, xb_s, xb_r, yc_s, yc_r, ys_s, ys_r, yb_s, yb_r,
):
    wide = lax.axis_index("wide")
    narrow = lax.axis_index("narrow")
    right = lax.rem(wide + 1, nw)
    left = lax.rem(wide + nw - 1, nw)
    upper = lax.rem(narrow + 1, nn)
    lower = lax.rem(narrow + nn - 1, nn)
    zt = pot.shape[2] // LANES
    pad = (buf_a.shape[1] - nw) // 2

    barrier = pltpu.get_barrier_semaphore()

    def greet_wide(k, _):
        pl.semaphore_signal(
            barrier, inc=1, device_id={"wide": lax.rem(wide + k, nw)}, device_id_type=MESH
        )
        return 0

    def greet_narrow(k, _):
        pl.semaphore_signal(
            barrier, inc=1, device_id={"narrow": lax.rem(narrow + k, nn)}, device_id_type=MESH
        )
        return 0

    lax.fori_loop(1, nw, greet_wide, 0)
    lax.fori_loop(1, nn, greet_narrow, 0)

    fl = [(1 - solid[x]).astype(F32) for x in range(2)]
    act = [[fl[x] * conc[k, x] for x in range(2)] for k in range(2)]
    for k in range(2):
        sx_r[k] = act[k][1]
        sx_l[k] = act[k][0]
    sx_r[2] = vel[0, 1]
    sx_l[2] = vel[0, 0]
    for x in range(2):
        sx_r[3 + x] = pot[x]
        sx_l[3 + x] = pot[x]
        for k in range(2):
            sy_u[x, k : k + 1] = act[k][x][7:8]
            sy_d[x, k : k + 1] = act[k][x][0:1]
        sy_u[x, 2:3] = vel[1, x, 7:8]
        sy_d[x, 2:3] = vel[1, x, 0:1]
        sy_u[x, 3:5] = pot[x, 6:8]
        sy_d[x, 3:5] = pot[x, 0:2]
        sy_u[x, 5:6] = fl[x][7:8]
        sy_d[x, 5:6] = fl[x][0:1]
        sy_u[x, 6:8] = jnp.zeros((2, pot.shape[2]), F32)
        sy_d[x, 6:8] = jnp.zeros((2, pot.shape[2]), F32)
    nothing = jnp.zeros((pad, ROWS, LANES), F32)
    for buf in (buf_a, buf_b):
        for k in range(3):
            buf[k, pl.ds(0, pad)] = nothing
            buf[k, pl.ds(pad + nw, pad)] = nothing
    xr[pl.ds(0, 1)] = nothing[:1]
    xr[pl.ds(nw + 1, 1)] = nothing[:1]

    def pack(row, v):
        for t in range(zt):
            packed[pl.ds((t * ROWS + row) * ROWS, ROWS), :] = v[:, t * LANES : (t + 1) * LANES]

    def to_stage(first):
        for t in range(zt):
            for y in range(ROWS):
                rows = packed[pl.ds((t * ROWS + first) * ROWS + y, 4, stride=ROWS), :]
                stage[y * zt + t, first : first + 4] = rows

    for x in range(2):
        charge = act[0][x] - act[1][x] + (1.0 - fl[x]) * fixed[x]
        pack(4 + x, pot[x] + 2.0 * charge)
        pack(6 + x, fl[x])
    to_stage(4)

    def over(axis, count, me, src, dst, send, recv):
        def leaving(k):
            peer = lax.rem(me + k, count)
            return pltpu.make_async_remote_copy(
                src_ref=src(peer), dst_ref=dst(me), send_sem=send.at[peer], recv_sem=recv.at[me],
                device_id={axis: peer}, device_id_type=MESH,
            )

        def arriving(k):
            peer = lax.rem(me + k, count)
            return pltpu.make_async_remote_copy(
                src_ref=src(peer), dst_ref=dst(peer), send_sem=send.at[peer], recv_sem=recv.at[peer],
                device_id={axis: peer}, device_id_type=MESH,
            )

        def run(copy_of, act_on):
            def body(k, _):
                act_on(copy_of(k))
                return 0

            lax.fori_loop(1, count, body, 0)

        return (
            lambda: run(leaving, lambda c: c.start()),
            lambda: run(arriving, lambda c: c.wait_recv()),
            lambda: run(leaving, lambda c: c.wait_send()),
        )

    def across_wide(src, dst, send, recv):
        return over("wide", nw, wide, src, dst, send, recv)

    def across_narrow(src, dst, send, recv):
        return over("narrow", nn, narrow, src, dst, send, recv)

    early = across_wide(
        lambda j: stage.at[j, pl.ds(4, 4)], lambda j: xr.at[j + 1, pl.ds(4, 4)], xe_s, xe_r
    )
    late = across_wide(
        lambda j: stage.at[j, pl.ds(0, 4)], lambda j: xr.at[j + 1, pl.ds(0, 4)], xs_s, xs_r
    )
    back = across_wide(
        lambda j: xsol.at[j, pl.ds(0, 6)], lambda j: xback.at[j, pl.ds(0, 6)], xb_s, xb_r
    )
    edges = across_narrow(lambda j: edge_s.at[j], lambda j: edge_r.at[j], yc_s, yc_r)
    datum = across_narrow(lambda j: dat_s.at[j], lambda j: dat_r.at[j], ys_s, ys_r)
    ends = across_narrow(lambda j: ends_s.at[j], lambda j: ends_r.at[j], yb_s, yb_r)

    pl.semaphore_wait(barrier, nw + nn - 2)

    halos = [
        pltpu.make_async_remote_copy(
            src_ref=src, dst_ref=dst, send_sem=hs.at[n], recv_sem=hr.at[n],
            device_id=peer, device_id_type=MESH,
        )
        for n, (src, dst, peer) in enumerate(
            (
                (sx_r, rx_l, {"wide": right}),
                (sx_l, rx_r, {"wide": left}),
                (sy_u, ry_d, {"narrow": upper}),
                (sy_d, ry_u, {"narrow": lower}),
            )
        )
    ]
    for copy in halos:
        copy.start()
    early[0]()

    shape = (ROWS, pot.shape[2])
    lane = lax.broadcasted_iota(jnp.int32, shape, 1)
    sub = lax.broadcasted_iota(jnp.int32, shape, 0)
    length = pot.shape[2]

    def z_next(v):
        return jnp.where(lane == length - 1, 0.0, pltpu.roll(v, length - 1, 1))

    def z_prev(v):
        return jnp.where(lane == 0, 0.0, pltpu.roll(v, 1, 1))

    def y_next(v, edge):
        return jnp.where(sub == ROWS - 1, edge, pltpu.roll(v, ROWS - 1, 0))

    def y_prev(v, edge):
        return jnp.where(sub == 0, edge, pltpu.roll(v, 1, 0))

    tilt = (0.125, -0.125)
    div_z = []
    for x in range(2):
        p = pot[x]
        slope = z_next(p) - z_prev(p)
        row = []
        for k in range(2):
            q = act[k][x] * (vel[2, x] - tilt[k] * slope)
            row.append((z_next(q) - z_prev(q)) * 0.5)
        div_z.append(row)

    for copy in halos:
        copy.wait()

    has_left = wide > 0
    has_right = wide < nw - 1
    has_down = narrow > 0
    has_up = narrow < nn - 1

    def kept(flag, v):
        return jnp.where(flag, v, 0.0)

    pots = [
        kept(has_left, rx_l[3]), kept(has_left, rx_l[4]), pot[0], pot[1],
        kept(has_right, rx_r[3]), kept(has_right, rx_r[4]),
    ]
    velx = [rx_l[2], vel[0, 0], vel[0, 1], rx_r[2]]
    for x in range(2):
        p = pot[x]
        down = kept(has_down, ry_d[x])
        up = kept(has_up, ry_u[x])
        slope_y = y_next(p, up[3:4]) - y_prev(p, down[4:5])
        slope_d = p[0:1] - down[3:4]
        slope_u = up[4:5] - p[7:8]
        for k in range(2):
            acts = [kept(has_left, rx_l[k]), act[k][0], act[k][1], kept(has_right, rx_r[k])]

            def flux_x(n):
                return acts[n] * (velx[n] - tilt[k] * (pots[n + 2] - pots[n]))

            div_x = (flux_x(x + 2) - flux_x(x)) * 0.5
            qy = act[k][x] * (vel[1, x] - tilt[k] * slope_y)
            q_down = down[k : k + 1] * (down[2:3] - tilt[k] * slope_d)
            q_up = up[k : k + 1] * (up[2:3] - tilt[k] * slope_u)
            div_y = (y_next(qy, q_up) - y_prev(qy, q_down)) * 0.5
            total = div_x + div_y + div_z[x][k]
            pack(2 * k + x, fl[x] * (conc[k, x] - 0.5 * total))
    to_stage(0)
    late[0]()
    xr[pl.ds(wide + 1, 1)] = stage[pl.ds(wide, 1)]

    even, is_pot, rate = row_facts()

    def y_rows(y):
        return pl.ds(y * zt, zt)

    def y_mask(y):
        if 0 <= y < ROWS:
            m0, m1 = masks(stage[y_rows(y)])
        else:
            halo, flag = (ry_d, has_down) if y < 0 else (ry_u, has_up)

            def lanes(x):
                row = kept(flag, halo[x, 5:6])
                return jnp.stack([row[:, t * LANES : (t + 1) * LANES] for t in range(zt)])

            m0, m1 = lanes(0), lanes(1)
        return jnp.where(is_pot, 1.0, jnp.where(even, m0, m1))

    before, here = y_mask(-1), y_mask(0)
    c_prev = left_prev = None
    for y in range(ROWS):
        after = y_mask(y + 1)
        rm = rate * here
        lower = -rm * before
        upper = -rm * after
        if y == 0:
            lower = kept(has_down, lower)
        if y == ROWS - 1:
            upper = kept(has_up, upper)
        main = 1.0 + rm * (before + after)
        if y == 0:
            m = 1.0 / main
            left_now = -lower * m
        else:
            m = 1.0 / (main - lower * c_prev)
            left_now = -lower * left_prev * m
        y_m[y_rows(y)] = m
        y_am[y_rows(y)] = lower * m
        c_prev, left_prev = upper * m, left_now
        y_c[y_rows(y)] = c_prev
        y_left[y_rows(y)] = left_now
        before, here = here, after
    right_now = -c_prev
    y_right[y_rows(ROWS - 1)] = right_now
    edge_s[:, 2] = left_prev
    edge_s[:, 3] = right_now
    for y in range(ROWS - 2, -1, -1):
        c_now = y_c[y_rows(y)]
        left_prev = y_left[y_rows(y)] - c_now * left_prev
        right_now = -c_now * right_now
        y_left[y_rows(y)] = left_prev
        y_right[y_rows(y)] = right_now
    edge_s[:, 0] = left_prev
    edge_s[:, 1] = right_now
    edges[0]()
    edge_r[pl.ds(narrow, 1)] = edge_s[pl.ds(narrow, 1)]

    early[1]()
    late[1]()
    solve_tiles(xr, 1, (buf_a, buf_b), xsol, 0, nw, pad, True)
    back[0]()
    xback[pl.ds(wide, 1)] = xsol[pl.ds(wide, 1)]

    edges[1]()
    gain = jnp.zeros((ROWS, LANES), F32)
    for n in range(nn):
        first_left, first_right, last_left, last_right = (edge_r[n, i] for i in range(4))
        q = 1.0 / (1.0 - first_left * gain)
        ring[n, 0] = q
        ring[n, 1] = q * first_left
        ring[n, 2] = last_left * gain
        ring[n, 3] = q * first_right
        gain = last_right + last_left * gain * (q * first_right)
        ring[n, 4] = gain

    back[1]()
    d = xback[y_rows(0)] * y_m[y_rows(0)]
    y_sol[y_rows(0)] = d
    for y in range(1, ROWS):
        d = xback[y_rows(y)] * y_m[y_rows(y)] - y_am[y_rows(y)] * d
        y_sol[y_rows(y)] = d
    dat_s[:, 1] = d
    for y in range(ROWS - 2, -1, -1):
        d = y_sol[y_rows(y)] - y_c[y_rows(y)] * d
        y_sol[y_rows(y)] = d
    dat_s[:, 0] = d
    datum[0]()
    dat_r[pl.ds(narrow, 1)] = dat_s[pl.ds(narrow, 1)]
    datum[1]()
    firsts, lasts = [], []
    last = jnp.zeros((ROWS, LANES), F32)
    for n in range(nn):
        first = ring[n, 0] * dat_r[n, 0] + ring[n, 1] * last
        last = dat_r[n, 1] + edge_r[n, 2] * last + ring[n, 2] * first
        firsts.append(first)
        lasts.append(last)
    following = jnp.zeros((ROWS, LANES), F32)
    for n in range(nn - 1, -1, -1):
        ends_s[n, 1] = following
        following = firsts[n] + ring[n, 3] * following
        if n > 0:
            ends_s[n, 0] = lasts[n - 1] + ring[n - 1, 4] * following
        else:
            ends_s[n, 0] = jnp.zeros((ROWS, LANES), F32)
    ends[0]()
    ends_r[pl.ds(narrow, 1)] = ends_s[pl.ds(narrow, 1)]
    ends[1]()
    from_left, from_right = ends_r[:, 0], ends_r[:, 1]
    for y in range(ROWS):
        out[y_rows(y)] = (
            y_sol[y_rows(y)] + y_left[y_rows(y)] * from_left + y_right[y_rows(y)] * from_right
        )
    for exchange in (early, late, back, edges, datum, ends):
        exchange[2]()

def z_kernel(tiles, solid, new_conc, new_pot):
    length = solid.shape[2]
    shape = (ROWS, length)
    lane = lax.broadcasted_iota(jnp.int32, shape, 1)
    first = lane == 0
    last = lane == length - 1

    def source(row):
        return jnp.concatenate(
            [
                tiles[pl.ds(t * ROWS + row, ROWS, stride=length // LANES * ROWS), :]
                for t in range(length // LANES)
            ],
            axis=1,
        )

    def solve(lower, upper, sources):
        spacing = 1
        while spacing < length:
            lower_prev, upper_prev = (pltpu.roll(v, spacing, 1) for v in (lower, upper))
            lower_next, upper_next = (pltpu.roll(v, length - spacing, 1) for v in (lower, upper))
            r = 1.0 / (1.0 - lower * upper_prev - upper * lower_next)
            sources = [
                (d - lower * pltpu.roll(d, spacing, 1) - upper * pltpu.roll(d, length - spacing, 1)) * r
                for d in sources
            ]
            lower, upper = -(lower * lower_prev) * r, -(upper * upper_next) * r
            spacing *= 2
        return sources

    for x in range(2):
        mask = (1 - solid[x]).astype(F32)
        before = jnp.where(first, 0.0, pltpu.roll(mask, 1, 1))
        after = jnp.where(last, 0.0, pltpu.roll(mask, length - 1, 1))
        for k, rate in enumerate((8.0, 5.0)):
            rm = rate * mask
            inv = 1.0 / (1.0 + rm * (before + after))
            (result,) = solve(
                -rm * before * inv, -rm * after * inv, [source(2 * k + x) * inv]
            )
            new_conc[k, x] = result
    inv = 1.0 / 33.0
    results = solve(
        jnp.where(first, 0.0, -16.0 * inv) * jnp.ones(shape, F32),
        jnp.where(last, 0.0, -16.0 * inv) * jnp.ones(shape, F32),
        [source(4) / 33.0, source(5) / 33.0],
    )
    for x in range(2):
        new_pot[x] = results[x]


def solution(mesh):
    nw, nn = mesh.shape["wide"], mesh.shape["narrow"]

    def shards(conc, potential, velocity, solid, fixed_charge):
        height = potential.shape[2]
        vmem = pl.BlockSpec(memory_space=pltpu.VMEM)
        tiles = (nw, ROWS, LANES)
        padded = (nw + 2, ROWS, LANES)
        plane = (5, ROWS, height)
        edge = (2, ROWS, height)
        bands = (3, 2 * nw, ROWS, LANES)
        dma = pltpu.SemaphoreType.DMA

        def body(*refs):
            main_kernel(nw, nn, *refs)

        after_y = pl.pallas_call(
            body,
            name="halo_x_y",
            out_shape=jax.ShapeDtypeStruct(tiles, F32),
            in_specs=[vmem] * 5,
            out_specs=vmem,
            scratch_shapes=[pltpu.VMEM(plane, F32)] * 4
            + [pltpu.VMEM(edge, F32)] * 4
            + [pltpu.VMEM((nw * ROWS, LANES), F32)]
            + [pltpu.VMEM(s, F32) for s in (tiles, padded, tiles, tiles, bands, bands)]
            + [pltpu.VMEM(tiles, F32)] * 6
            + [pltpu.VMEM((nn, n, ROWS, LANES), F32) for n in (4, 4, 2, 2, 2, 2, 5)]
            + [dma((4,))] * 2
            + [dma((nw,))] * 6
            + [dma((nn,))] * 6,
            compiler_params=pltpu.CompilerParams(collective_id=0, has_side_effects=True),
        )(conc, potential, velocity, solid, fixed_charge)
        return pl.pallas_call(
            z_kernel,
            name="solve_z",
            out_shape=(
                jax.ShapeDtypeStruct(conc.shape, F32),
                jax.ShapeDtypeStruct(potential.shape, F32),
            ),
            in_specs=[vmem] * 2,
            out_specs=(vmem, vmem),
        )(after_y.reshape(nw * ROWS, LANES), solid)

    return jax.shard_map(
        shards,
        mesh=mesh,
        in_specs=(
            P(None, "wide", "narrow", None),
            P("wide", "narrow", None),
            P(None, "wide", "narrow", None),
            P("wide", "narrow", None),
            P("wide", "narrow", None),
        ),
        out_specs=(P(None, "wide", "narrow", None), P("wide", "narrow", None)),
        check_vma=False,
    )
```

```python
import jax
import jax.numpy as jnp
from jax import lax
from jax.experimental import pallas as pl
from jax.experimental.pallas import tpu as pltpu
from jax.sharding import PartitionSpec as P

F32 = jnp.float32
MESH = pl.DeviceIdType.MESH
LANES = 128
ROWS = 8
CHUNK = 8


def pcr(here, prev, succ):
    a, c, d = here
    ap, cp, dp = prev
    an, cn, dn = succ
    r = 1.0 / (1.0 - a * cp - c * an)
    return -(a * ap) * r, -(c * cn) * r, (d - a * dp - c * dn) * r


def row_facts():
    row = lax.broadcasted_iota(jnp.int32, (1, ROWS, LANES), 1)
    even = row % 2 == 0
    is_pot = row >= 4
    rate = jnp.where(row < 2, 8.0, jnp.where(row < 4, 5.0, jnp.where(row < 6, 16.0, 0.0)))
    return even, is_pot, rate.astype(F32)


def masks(tiles):
    return tiles[:, 6:7, :], tiles[:, 7:8, :]


def normal_bands(tiles, mask, mask_prev, mask_next, rate, is_first, is_last):
    rm = rate * mask
    inv = 1.0 / (1.0 + rm * (mask_prev + mask_next))
    lower = jnp.where(is_first, 0.0, -rm * mask_prev * inv)
    upper = jnp.where(is_last, 0.0, -rm * mask_next * inv)
    return lower, upper, tiles * inv


def solve_tiles(src_ref, src_pad, bufs, dst_ref, dst_pad, count, pad, paired):
    def build(i, _):
        even, is_pot, rate = row_facts()
        base = src_pad + i * CHUNK
        tiles = src_ref[pl.ds(base, CHUNK)]
        m0, m1 = masks(tiles)
        p0, p1 = masks(src_ref[pl.ds(base - 1, CHUNK)])
        n0, n1 = masks(src_ref[pl.ds(base + 1, CHUNK)])
        own = jnp.where(is_pot, 1.0, jnp.where(even, m0, m1))
        place = i * CHUNK + lax.broadcasted_iota(jnp.int32, (CHUNK, ROWS, LANES), 0)
        first = place == 0
        last = place == count - 1
        if paired:
            before = jnp.where(is_pot, 1.0, jnp.where(even, p1, m0))
            after = jnp.where(is_pot, 1.0, jnp.where(even, m1, n0))
            first = first & even
            last = last & jnp.logical_not(even)
        else:
            before = jnp.where(is_pot, 1.0, jnp.where(even, p0, p1))
            after = jnp.where(is_pot, 1.0, jnp.where(even, n0, n1))
        bands = normal_bands(tiles, own, before, after, rate, first, last)
        for k in range(3):
            bufs[0][k, pl.ds(pad + i * CHUNK, CHUNK)] = bands[k]
        return 0

    lax.fori_loop(0, count // CHUNK, build, 0)
    now = 0

    def window(buf, base):
        return tuple(buf[k, pl.ds(base, CHUNK)] for k in range(3))

    if paired:

        def pair_step(i, _):
            even, _, _ = row_facts()
            base = pad + i * CHUNK
            here = window(bufs[0], base)
            left = window(bufs[0], base - 1)
            right = window(bufs[0], base + 1)

            def up(v):
                return pltpu.roll(v, ROWS - 1, 1)

            def down(v):
                return pltpu.roll(v, 1, 1)

            prev = tuple(jnp.where(even, up(l), down(h)) for l, h in zip(left, here))
            succ = tuple(jnp.where(even, up(h), down(r)) for h, r in zip(here, right))
            for k, v in enumerate(pcr(here, prev, succ)):
                bufs[1][k, pl.ds(base, CHUNK)] = v
            return 0

        lax.fori_loop(0, count // CHUNK, pair_step, 0)
        now = 1

    spacing = 1
    while spacing < count:
        source, target = bufs[now], bufs[1 - now]
        final = spacing * 2 >= count

        def step(i, _, source=source, target=target, spacing=spacing, final=final):
            base = pad + i * CHUNK
            new = pcr(
                window(source, base), window(source, base - spacing), window(source, base + spacing)
            )
            if final:
                dst_ref[pl.ds(dst_pad + i * CHUNK, CHUNK)] = new[2]
            else:
                for k in range(3):
                    target[k, pl.ds(base, CHUNK)] = new[k]
            return 0

        lax.fori_loop(0, count // CHUNK, step, 0)
        now = 1 - now
        spacing *= 2


def z_reduce(solid, z_inv, z_steps, length):
    shape = (ROWS, length)
    lane = lax.broadcasted_iota(jnp.int32, shape, 1)
    for case in range(5):
        if case < 4:
            rm = (8.0, 5.0)[case // 2] * (1 - solid[case % 2]).astype(F32)
            mask = (1 - solid[case % 2]).astype(F32)
            before = jnp.where(lane == 0, 0.0, pltpu.roll(mask, 1, 1))
            after = jnp.where(lane == length - 1, 0.0, pltpu.roll(mask, length - 1, 1))
            inv = 1.0 / (1.0 + rm * (before + after))
            lower, upper = -rm * before * inv, -rm * after * inv
        else:
            inv = jnp.full(shape, 1.0 / 33.0, F32)
            lower = jnp.where(lane == 0, 0.0, -16.0 * inv)
            upper = jnp.where(lane == length - 1, 0.0, -16.0 * inv)
        z_inv[case] = inv
        spacing, step = 1, 0
        while spacing < length:
            lower_prev, upper_prev = (pltpu.roll(v, spacing, 1) for v in (lower, upper))
            lower_next, upper_next = (pltpu.roll(v, length - spacing, 1) for v in (lower, upper))
            r = 1.0 / (1.0 - lower * upper_prev - upper * lower_next)
            lower, upper = lower * r, upper * r
            for k, v in enumerate((r, lower, upper)):
                z_steps[case, step, k] = v
            lower, upper = -lower * lower_prev, -upper * upper_next
            spacing, step = spacing * 2, step + 1


def z_solve(packed, field, z_inv, z_steps, length):
    cases = [min(2 * field + x, 4) for x in range(2)]
    values = []
    for x in range(2):
        parts = [
            packed[pl.ds((t * ROWS + 2 * field + x) * ROWS, ROWS), :] for t in range(length // LANES)
        ]
        values.append(jnp.concatenate(parts, axis=1) * z_inv[cases[x]])
    spacing, step = 1, 0
    while spacing < length:
        for x in range(2):
            d = values[x]
            r, lower, upper = (z_steps[cases[x], step, k] for k in range(3))
            values[x] = (
                d * r - lower * pltpu.roll(d, spacing, 1) - upper * pltpu.roll(d, length - spacing, 1)
            )
        spacing, step = spacing * 2, step + 1
    return values


def main_kernel(
    nw, nn, conc, pot, vel, solid, fixed, new_conc, new_pot,
    sx_r, sx_l, rx_l, rx_r, sy_u, sy_d, ry_d, ry_u, packed, stage, xr, xsol, xback,
    buf_a, buf_b, y_am, y_m, y_c, y_left, y_right, y_sol,
    edge_s, edge_r, dat_s, dat_r, ends_s, ends_r, ring, z_inv, z_steps,
    hs, hr, xs_s, xs_r, xb_s, xb_r, yc_s, yc_r, ys_s, ys_r, yb_s, yb_r,
):
    wide = lax.axis_index("wide")
    narrow = lax.axis_index("narrow")
    right = lax.rem(wide + 1, nw)
    left = lax.rem(wide + nw - 1, nw)
    upper = lax.rem(narrow + 1, nn)
    lower = lax.rem(narrow + nn - 1, nn)
    zt = pot.shape[2] // LANES
    pad = (buf_a.shape[1] - nw) // 2

    barrier = pltpu.get_barrier_semaphore()

    def greet_wide(k, _):
        pl.semaphore_signal(
            barrier, inc=1, device_id={"wide": lax.rem(wide + k, nw)}, device_id_type=MESH
        )
        return 0

    def greet_narrow(k, _):
        pl.semaphore_signal(
            barrier, inc=1, device_id={"narrow": lax.rem(narrow + k, nn)}, device_id_type=MESH
        )
        return 0

    lax.fori_loop(1, nw, greet_wide, 0)
    lax.fori_loop(1, nn, greet_narrow, 0)

    fl = [(1 - solid[x]).astype(F32) for x in range(2)]
    act = [[fl[x] * conc[k, x] for x in range(2)] for k in range(2)]
    for k in range(2):
        sx_r[k] = act[k][1]
        sx_l[k] = act[k][0]
    sx_r[2] = vel[0, 1]
    sx_l[2] = vel[0, 0]
    for x in range(2):
        sx_r[3 + x] = pot[x]
        sx_l[3 + x] = pot[x]
        for k in range(2):
            sy_u[x, k : k + 1] = act[k][x][7:8]
            sy_d[x, k : k + 1] = act[k][x][0:1]
        sy_u[x, 2:3] = vel[1, x, 7:8]
        sy_d[x, 2:3] = vel[1, x, 0:1]
        sy_u[x, 3:5] = pot[x, 6:8]
        sy_d[x, 3:5] = pot[x, 0:2]
        sy_u[x, 5:6] = fl[x][7:8]
        sy_d[x, 5:6] = fl[x][0:1]
        sy_u[x, 6:8] = jnp.zeros((2, pot.shape[2]), F32)
        sy_d[x, 6:8] = jnp.zeros((2, pot.shape[2]), F32)
    nothing = jnp.zeros((pad, ROWS, LANES), F32)
    for buf in (buf_a, buf_b):
        for k in range(3):
            buf[k, pl.ds(0, pad)] = nothing
            buf[k, pl.ds(pad + nw, pad)] = nothing
    xr[pl.ds(0, 1)] = nothing[:1]
    xr[pl.ds(nw + 1, 1)] = nothing[:1]

    def pack(row, v):
        for t in range(zt):
            packed[pl.ds((t * ROWS + row) * ROWS, ROWS), :] = v[:, t * LANES : (t + 1) * LANES]

    def to_stage(first):
        for t in range(zt):
            for y in range(ROWS):
                rows = packed[pl.ds((t * ROWS + first) * ROWS + y, 4, stride=ROWS), :]
                stage[y * zt + t, first : first + 4] = rows

    for x in range(2):
        charge = act[0][x] - act[1][x] + (1.0 - fl[x]) * fixed[x]
        pack(4 + x, pot[x] + 2.0 * charge)
        pack(6 + x, fl[x])
    to_stage(4)

    def over(axis, count, me, src, dst, send, recv):
        def leaving(k):
            peer = lax.rem(me + k, count)
            return pltpu.make_async_remote_copy(
                src_ref=src(peer), dst_ref=dst(me), send_sem=send.at[peer], recv_sem=recv.at[me],
                device_id={axis: peer}, device_id_type=MESH,
            )

        def arriving(k):
            peer = lax.rem(me + k, count)
            return pltpu.make_async_remote_copy(
                src_ref=src(peer), dst_ref=dst(peer), send_sem=send.at[peer], recv_sem=recv.at[peer],
                device_id={axis: peer}, device_id_type=MESH,
            )

        def run(copy_of, act_on):
            def body(k, _):
                act_on(copy_of(k))
                return 0

            lax.fori_loop(1, count, body, 0)

        return (
            lambda: run(leaving, lambda c: c.start()),
            lambda: run(arriving, lambda c: c.wait_recv()),
            lambda: run(leaving, lambda c: c.wait_send()),
        )

    def across_wide(src, dst, send, recv):
        return over("wide", nw, wide, src, dst, send, recv)

    def across_narrow(src, dst, send, recv):
        return over("narrow", nn, narrow, src, dst, send, recv)

    lines = across_wide(lambda j: stage.at[j], lambda j: xr.at[j + 1], xs_s, xs_r)
    back = across_wide(
        lambda j: xsol.at[j, pl.ds(0, 6)], lambda j: xback.at[j, pl.ds(0, 6)], xb_s, xb_r
    )
    edges = across_narrow(lambda j: edge_s.at[j], lambda j: edge_r.at[j], yc_s, yc_r)
    datum = across_narrow(lambda j: dat_s.at[j], lambda j: dat_r.at[j], ys_s, ys_r)
    ends = across_narrow(lambda j: ends_s.at[j], lambda j: ends_r.at[j], yb_s, yb_r)

    pl.semaphore_wait(barrier, nw + nn - 2)

    halos = [
        pltpu.make_async_remote_copy(
            src_ref=src, dst_ref=dst, send_sem=hs.at[n], recv_sem=hr.at[n],
            device_id=peer, device_id_type=MESH,
        )
        for n, (src, dst, peer) in enumerate(
            (
                (sx_r, rx_l, {"wide": right}),
                (sx_l, rx_r, {"wide": left}),
                (sy_u, ry_d, {"narrow": upper}),
                (sy_d, ry_u, {"narrow": lower}),
            )
        )
    ]
    for copy in halos:
        copy.start()

    shape = (ROWS, pot.shape[2])
    lane = lax.broadcasted_iota(jnp.int32, shape, 1)
    sub = lax.broadcasted_iota(jnp.int32, shape, 0)
    length = pot.shape[2]

    def z_next(v):
        return jnp.where(lane == length - 1, 0.0, pltpu.roll(v, length - 1, 1))

    def z_prev(v):
        return jnp.where(lane == 0, 0.0, pltpu.roll(v, 1, 1))

    def y_next(v, edge):
        return jnp.where(sub == ROWS - 1, edge, pltpu.roll(v, ROWS - 1, 0))

    def y_prev(v, edge):
        return jnp.where(sub == 0, edge, pltpu.roll(v, 1, 0))

    tilt = (0.125, -0.125)
    div_z = []
    for x in range(2):
        p = pot[x]
        slope = z_next(p) - z_prev(p)
        row = []
        for k in range(2):
            q = act[k][x] * (vel[2, x] - tilt[k] * slope)
            row.append((z_next(q) - z_prev(q)) * 0.5)
        div_z.append(row)

    for copy in halos:
        copy.wait()

    has_left = wide > 0
    has_right = wide < nw - 1
    has_down = narrow > 0
    has_up = narrow < nn - 1

    def kept(flag, v):
        return jnp.where(flag, v, 0.0)

    pots = [
        kept(has_left, rx_l[3]), kept(has_left, rx_l[4]), pot[0], pot[1],
        kept(has_right, rx_r[3]), kept(has_right, rx_r[4]),
    ]
    velx = [rx_l[2], vel[0, 0], vel[0, 1], rx_r[2]]
    for x in range(2):
        p = pot[x]
        down = kept(has_down, ry_d[x])
        up = kept(has_up, ry_u[x])
        slope_y = y_next(p, up[3:4]) - y_prev(p, down[4:5])
        slope_d = p[0:1] - down[3:4]
        slope_u = up[4:5] - p[7:8]
        for k in range(2):
            acts = [kept(has_left, rx_l[k]), act[k][0], act[k][1], kept(has_right, rx_r[k])]

            def flux_x(n):
                return acts[n] * (velx[n] - tilt[k] * (pots[n + 2] - pots[n]))

            div_x = (flux_x(x + 2) - flux_x(x)) * 0.5
            qy = act[k][x] * (vel[1, x] - tilt[k] * slope_y)
            q_down = down[k : k + 1] * (down[2:3] - tilt[k] * slope_d)
            q_up = up[k : k + 1] * (up[2:3] - tilt[k] * slope_u)
            div_y = (y_next(qy, q_up) - y_prev(qy, q_down)) * 0.5
            total = div_x + div_y + div_z[x][k]
            pack(2 * k + x, fl[x] * (conc[k, x] - 0.5 * total))
    to_stage(0)
    lines[0]()
    xr[pl.ds(wide + 1, 1)] = stage[pl.ds(wide, 1)]

    even, is_pot, rate = row_facts()

    def y_rows(y):
        return pl.ds(y * zt, zt)

    def y_mask(y):
        if 0 <= y < ROWS:
            m0, m1 = masks(stage[y_rows(y)])
        else:
            halo, flag = (ry_d, has_down) if y < 0 else (ry_u, has_up)

            def lanes(x):
                row = kept(flag, halo[x, 5:6])
                return jnp.stack([row[:, t * LANES : (t + 1) * LANES] for t in range(zt)])

            m0, m1 = lanes(0), lanes(1)
        return jnp.where(is_pot, 1.0, jnp.where(even, m0, m1))

    before, here = y_mask(-1), y_mask(0)
    c_prev = left_prev = None
    for y in range(ROWS):
        after = y_mask(y + 1)
        rm = rate * here
        lower = -rm * before
        upper = -rm * after
        if y == 0:
            lower = kept(has_down, lower)
        if y == ROWS - 1:
            upper = kept(has_up, upper)
        main = 1.0 + rm * (before + after)
        if y == 0:
            m = 1.0 / main
            left_now = -lower * m
        else:
            m = 1.0 / (main - lower * c_prev)
            left_now = -lower * left_prev * m
        y_m[y_rows(y)] = m
        y_am[y_rows(y)] = lower * m
        c_prev, left_prev = upper * m, left_now
        y_c[y_rows(y)] = c_prev
        y_left[y_rows(y)] = left_now
        before, here = here, after
    right_now = -c_prev
    y_right[y_rows(ROWS - 1)] = right_now
    edge_s[:, 2] = left_prev
    edge_s[:, 3] = right_now
    for y in range(ROWS - 2, -1, -1):
        c_now = y_c[y_rows(y)]
        left_prev = y_left[y_rows(y)] - c_now * left_prev
        right_now = -c_now * right_now
        y_left[y_rows(y)] = left_prev
        y_right[y_rows(y)] = right_now
    edge_s[:, 0] = left_prev
    edge_s[:, 1] = right_now
    edges[0]()
    edge_r[pl.ds(narrow, 1)] = edge_s[pl.ds(narrow, 1)]

    lines[1]()
    solve_tiles(xr, 1, (buf_a, buf_b), xsol, 0, nw, pad, True)
    back[0]()
    xback[pl.ds(wide, 1)] = xsol[pl.ds(wide, 1)]
    z_reduce(solid, z_inv, z_steps, length)

    edges[1]()
    gain = jnp.zeros((ROWS, LANES), F32)
    for n in range(nn):
        first_left, first_right, last_left, last_right = (edge_r[n, i] for i in range(4))
        q = 1.0 / (1.0 - first_left * gain)
        ring[n, 0] = q
        ring[n, 1] = q * first_left
        ring[n, 2] = last_left * gain
        ring[n, 3] = q * first_right
        gain = last_right + last_left * gain * (q * first_right)
        ring[n, 4] = gain

    back[1]()
    d = xback[y_rows(0)] * y_m[y_rows(0)]
    y_sol[y_rows(0)] = d
    for y in range(1, ROWS):
        d = xback[y_rows(y)] * y_m[y_rows(y)] - y_am[y_rows(y)] * d
        y_sol[y_rows(y)] = d
    dat_s[:, 1] = d
    for y in range(ROWS - 2, -1, -1):
        d = y_sol[y_rows(y)] - y_c[y_rows(y)] * d
        y_sol[y_rows(y)] = d
    dat_s[:, 0] = d
    datum[0]()
    dat_r[pl.ds(narrow, 1)] = dat_s[pl.ds(narrow, 1)]
    datum[1]()
    firsts, lasts = [], []
    last = jnp.zeros((ROWS, LANES), F32)
    for n in range(nn):
        first = ring[n, 0] * dat_r[n, 0] + ring[n, 1] * last
        last = dat_r[n, 1] + edge_r[n, 2] * last + ring[n, 2] * first
        firsts.append(first)
        lasts.append(last)
    following = jnp.zeros((ROWS, LANES), F32)
    for n in range(nn - 1, -1, -1):
        ends_s[n, 1] = following
        following = firsts[n] + ring[n, 3] * following
        if n > 0:
            ends_s[n, 0] = lasts[n - 1] + ring[n - 1, 4] * following
        else:
            ends_s[n, 0] = jnp.zeros((ROWS, LANES), F32)
    ends[0]()
    ends_r[pl.ds(narrow, 1)] = ends_s[pl.ds(narrow, 1)]
    ends[1]()
    from_left, from_right = ends_r[:, 0], ends_r[:, 1]
    for y in range(ROWS):
        value = y_sol[y_rows(y)] + y_left[y_rows(y)] * from_left + y_right[y_rows(y)] * from_right
        for t in range(zt):
            packed[pl.ds(t * ROWS * ROWS + y, ROWS, stride=ROWS), :] = value[t]
    for k in range(3):
        for x, value in enumerate(z_solve(packed, k, z_inv, z_steps, length)):
            if k < 2:
                new_conc[k, x] = value
            else:
                new_pot[x] = value
    for exchange in (lines, back, edges, datum, ends):
        exchange[2]()

def solution(mesh):
    nw, nn = mesh.shape["wide"], mesh.shape["narrow"]

    def shards(conc, potential, velocity, solid, fixed_charge):
        height = potential.shape[2]
        vmem = pl.BlockSpec(memory_space=pltpu.VMEM)
        tiles = (nw, ROWS, LANES)
        padded = (nw + 2, ROWS, LANES)
        plane = (5, ROWS, height)
        edge = (2, ROWS, height)
        bands = (3, 2 * nw, ROWS, LANES)
        dma = pltpu.SemaphoreType.DMA

        def body(*refs):
            main_kernel(nw, nn, *refs)

        return pl.pallas_call(
            body,
            name="adi_step",
            out_shape=(
                jax.ShapeDtypeStruct(conc.shape, F32),
                jax.ShapeDtypeStruct(potential.shape, F32),
            ),
            in_specs=[vmem] * 5,
            out_specs=(vmem, vmem),
            scratch_shapes=[pltpu.VMEM(plane, F32)] * 4
            + [pltpu.VMEM(edge, F32)] * 4
            + [pltpu.VMEM((nw * ROWS, LANES), F32)]
            + [pltpu.VMEM(s, F32) for s in (tiles, padded, tiles, tiles, bands, bands)]
            + [pltpu.VMEM(tiles, F32)] * 6
            + [pltpu.VMEM((nn, n, ROWS, LANES), F32) for n in (4, 4, 2, 2, 2, 2, 5)]
            + [pltpu.VMEM((5, ROWS, height), F32)]
            + [pltpu.VMEM((5, (height - 1).bit_length(), 3, ROWS, height), F32)]
            + [dma((4,))] * 2
            + [dma((nw,))] * 4
            + [dma((nn,))] * 6,
            compiler_params=pltpu.CompilerParams(collective_id=0, has_side_effects=True),
        )(conc, potential, velocity, solid, fixed_charge)

    return jax.shard_map(
        shards,
        mesh=mesh,
        in_specs=(
            P(None, "wide", "narrow", None),
            P("wide", "narrow", None),
            P(None, "wide", "narrow", None),
            P("wide", "narrow", None),
            P("wide", "narrow", None),
        ),
        out_specs=(P(None, "wide", "narrow", None), P("wide", "narrow", None)),
        check_vma=False,
    )
```

```python
import jax
import jax.numpy as jnp
from jax import lax
from jax.experimental import pallas as pl
from jax.experimental.pallas import tpu as pltpu
from jax.sharding import PartitionSpec as P

F32 = jnp.float32
MESH = pl.DeviceIdType.MESH
LANES = 128
ROWS = 8
CHUNK = 8


def pcr(here, prev, succ):
    a, c, d = here
    ap, cp, dp = prev
    an, cn, dn = succ
    r = 1.0 / (1.0 - a * cp - c * an)
    return -(a * ap) * r, -(c * cn) * r, (d - a * dp - c * dn) * r


def row_facts():
    row = lax.broadcasted_iota(jnp.int32, (1, ROWS, LANES), 1)
    even = row % 2 == 0
    is_pot = row >= 4
    rate = jnp.where(row < 2, 8.0, jnp.where(row < 4, 5.0, jnp.where(row < 6, 16.0, 0.0)))
    return even, is_pot, rate.astype(F32)


def masks(tiles):
    return tiles[:, 6:7, :], tiles[:, 7:8, :]


def normal_bands(tiles, mask, mask_prev, mask_next, rate, is_first, is_last):
    rm = rate * mask
    inv = 1.0 / (1.0 + rm * (mask_prev + mask_next))
    lower = jnp.where(is_first, 0.0, -rm * mask_prev * inv)
    upper = jnp.where(is_last, 0.0, -rm * mask_next * inv)
    return lower, upper, tiles * inv


def solve_tiles(src_ref, src_pad, bufs, dst_ref, dst_pad, count, pad, paired):
    def build(i, _):
        even, is_pot, rate = row_facts()
        base = src_pad + i * CHUNK
        tiles = src_ref[pl.ds(base, CHUNK)]
        m0, m1 = masks(tiles)
        p0, p1 = masks(src_ref[pl.ds(base - 1, CHUNK)])
        n0, n1 = masks(src_ref[pl.ds(base + 1, CHUNK)])
        own = jnp.where(is_pot, 1.0, jnp.where(even, m0, m1))
        place = i * CHUNK + lax.broadcasted_iota(jnp.int32, (CHUNK, ROWS, LANES), 0)
        first = place == 0
        last = place == count - 1
        if paired:
            before = jnp.where(is_pot, 1.0, jnp.where(even, p1, m0))
            after = jnp.where(is_pot, 1.0, jnp.where(even, m1, n0))
            first = first & even
            last = last & jnp.logical_not(even)
        else:
            before = jnp.where(is_pot, 1.0, jnp.where(even, p0, p1))
            after = jnp.where(is_pot, 1.0, jnp.where(even, n0, n1))
        bands = normal_bands(tiles, own, before, after, rate, first, last)
        for k in range(3):
            bufs[0][k, pl.ds(pad + i * CHUNK, CHUNK)] = bands[k]
        return 0

    lax.fori_loop(0, count // CHUNK, build, 0)
    now = 0

    def window(buf, base):
        return tuple(buf[k, pl.ds(base, CHUNK)] for k in range(3))

    if paired:

        def pair_step(i, _):
            even, _, _ = row_facts()
            base = pad + i * CHUNK
            here = window(bufs[0], base)
            left = window(bufs[0], base - 1)
            right = window(bufs[0], base + 1)

            def up(v):
                return pltpu.roll(v, ROWS - 1, 1)

            def down(v):
                return pltpu.roll(v, 1, 1)

            prev = tuple(jnp.where(even, up(l), down(h)) for l, h in zip(left, here))
            succ = tuple(jnp.where(even, up(h), down(r)) for h, r in zip(here, right))
            for k, v in enumerate(pcr(here, prev, succ)):
                bufs[1][k, pl.ds(base, CHUNK)] = v
            return 0

        lax.fori_loop(0, count // CHUNK, pair_step, 0)
        now = 1

    spacing = 1
    while spacing < count:
        source, target = bufs[now], bufs[1 - now]
        final = spacing * 2 >= count

        def step(i, _, source=source, target=target, spacing=spacing, final=final):
            base = pad + i * CHUNK
            new = pcr(
                window(source, base), window(source, base - spacing), window(source, base + spacing)
            )
            if final:
                dst_ref[pl.ds(dst_pad + i * CHUNK, CHUNK)] = new[2]
            else:
                for k in range(3):
                    target[k, pl.ds(base, CHUNK)] = new[k]
            return 0

        lax.fori_loop(0, count // CHUNK, step, 0)
        now = 1 - now
        spacing *= 2


def z_reduce(solid, z_inv, z_steps, length):
    shape = (ROWS, length)
    lane = lax.broadcasted_iota(jnp.int32, shape, 1)
    for case in range(5):
        if case < 4:
            rm = (8.0, 5.0)[case // 2] * (1 - solid[case % 2]).astype(F32)
            mask = (1 - solid[case % 2]).astype(F32)
            before = jnp.where(lane == 0, 0.0, pltpu.roll(mask, 1, 1))
            after = jnp.where(lane == length - 1, 0.0, pltpu.roll(mask, length - 1, 1))
            inv = 1.0 / (1.0 + rm * (before + after))
            lower, upper = -rm * before * inv, -rm * after * inv
        else:
            inv = jnp.full(shape, 1.0 / 33.0, F32)
            lower = jnp.where(lane == 0, 0.0, -16.0 * inv)
            upper = jnp.where(lane == length - 1, 0.0, -16.0 * inv)
        z_inv[case] = inv
        spacing, step = 1, 0
        while spacing < length:
            lower_prev, upper_prev = (pltpu.roll(v, spacing, 1) for v in (lower, upper))
            lower_next, upper_next = (pltpu.roll(v, length - spacing, 1) for v in (lower, upper))
            r = 1.0 / (1.0 - lower * upper_prev - upper * lower_next)
            lower, upper = lower * r, upper * r
            for k, v in enumerate((r, lower, upper)):
                z_steps[case, step, k] = v
            lower, upper = -lower * lower_prev, -upper * upper_next
            spacing, step = spacing * 2, step + 1


def z_solve(packed, field, z_inv, z_steps, length):
    cases = [min(2 * field + x, 4) for x in range(2)]
    values = []
    for x in range(2):
        parts = [
            packed[pl.ds((t * ROWS + 2 * field + x) * ROWS, ROWS), :] for t in range(length // LANES)
        ]
        values.append(jnp.concatenate(parts, axis=1) * z_inv[cases[x]])
    spacing, step = 1, 0
    while spacing < length:
        for x in range(2):
            d = values[x]
            r, lower, upper = (z_steps[cases[x], step, k] for k in range(3))
            values[x] = (
                d * r - lower * pltpu.roll(d, spacing, 1) - upper * pltpu.roll(d, length - spacing, 1)
            )
        spacing, step = spacing * 2, step + 1
    return values


def main_kernel(
    nw, nn, conc_in, pot_in, vel_in, solid_in, fixed_in, new_conc, new_pot,
    conc, pot, vel, solid, fixed, in_sem,
    sx_r, sx_l, rx_l, rx_r, sy_u, sy_d, ry_d, ry_u, packed, stage, xr, xsol, xback,
    buf_a, buf_b, y_am, y_m, y_c, y_left, y_right, y_sol,
    edge_s, edge_r, dat_s, dat_r, ends_s, ends_r, ring, z_inv, z_steps,
    hs, hr, xs_s, xs_r, xb_s, xb_r, yc_s, yc_r, ys_s, ys_r, yb_s, yb_r,
):
    wide = lax.axis_index("wide")
    narrow = lax.axis_index("narrow")
    right = lax.rem(wide + 1, nw)
    left = lax.rem(wide + nw - 1, nw)
    upper = lax.rem(narrow + 1, nn)
    lower = lax.rem(narrow + nn - 1, nn)
    zt = pot.shape[2] // LANES
    pad = (buf_a.shape[1] - nw) // 2

    loads = [
        pltpu.make_async_copy(src, dst, in_sem.at[n])
        for n, (src, dst) in enumerate(
            (
                (solid_in, solid), (conc_in, conc), (pot_in, pot), (vel_in, vel), (fixed_in, fixed)
            )
        )
    ]
    for load in loads:
        load.start()
    barrier = pltpu.get_barrier_semaphore()

    def greet_wide(k, _):
        pl.semaphore_signal(
            barrier, inc=1, device_id={"wide": lax.rem(wide + k, nw)}, device_id_type=MESH
        )
        return 0

    def greet_narrow(k, _):
        pl.semaphore_signal(
            barrier, inc=1, device_id={"narrow": lax.rem(narrow + k, nn)}, device_id_type=MESH
        )
        return 0

    lax.fori_loop(1, nw, greet_wide, 0)
    lax.fori_loop(1, nn, greet_narrow, 0)

    for load in loads:
        load.wait()
    fl = [(1 - solid[x]).astype(F32) for x in range(2)]
    act = [[fl[x] * conc[k, x] for x in range(2)] for k in range(2)]
    for k in range(2):
        sx_r[k] = act[k][1]
        sx_l[k] = act[k][0]
    sx_r[2] = vel[0, 1]
    sx_l[2] = vel[0, 0]
    for x in range(2):
        sx_r[3 + x] = pot[x]
        sx_l[3 + x] = pot[x]
        for k in range(2):
            sy_u[x, k : k + 1] = act[k][x][7:8]
            sy_d[x, k : k + 1] = act[k][x][0:1]
        sy_u[x, 2:3] = vel[1, x, 7:8]
        sy_d[x, 2:3] = vel[1, x, 0:1]
        sy_u[x, 3:5] = pot[x, 6:8]
        sy_d[x, 3:5] = pot[x, 0:2]
        sy_u[x, 5:6] = fl[x][7:8]
        sy_d[x, 5:6] = fl[x][0:1]
        sy_u[x, 6:8] = jnp.zeros((2, pot.shape[2]), F32)
        sy_d[x, 6:8] = jnp.zeros((2, pot.shape[2]), F32)
    nothing = jnp.zeros((pad, ROWS, LANES), F32)
    for buf in (buf_a, buf_b):
        for k in range(3):
            buf[k, pl.ds(0, pad)] = nothing
            buf[k, pl.ds(pad + nw, pad)] = nothing
    xr[pl.ds(0, 1)] = nothing[:1]
    xr[pl.ds(nw + 1, 1)] = nothing[:1]

    def pack(row, v):
        for t in range(zt):
            packed[pl.ds((t * ROWS + row) * ROWS, ROWS), :] = v[:, t * LANES : (t + 1) * LANES]

    def to_stage(first):
        for t in range(zt):
            for y in range(ROWS):
                rows = packed[pl.ds((t * ROWS + first) * ROWS + y, 4, stride=ROWS), :]
                stage[y * zt + t, first : first + 4] = rows

    for x in range(2):
        charge = act[0][x] - act[1][x] + (1.0 - fl[x]) * fixed[x]
        pack(4 + x, pot[x] + 2.0 * charge)
        pack(6 + x, fl[x])
    to_stage(4)

    def over(axis, count, me, src, dst, send, recv):
        def leaving(k):
            peer = lax.rem(me + k, count)
            return pltpu.make_async_remote_copy(
                src_ref=src(peer), dst_ref=dst(me), send_sem=send.at[peer], recv_sem=recv.at[me],
                device_id={axis: peer}, device_id_type=MESH,
            )

        def arriving(k):
            peer = lax.rem(me + k, count)
            return pltpu.make_async_remote_copy(
                src_ref=src(peer), dst_ref=dst(peer), send_sem=send.at[peer], recv_sem=recv.at[peer],
                device_id={axis: peer}, device_id_type=MESH,
            )

        def run(copy_of, act_on):
            def body(k, _):
                act_on(copy_of(k))
                return 0

            lax.fori_loop(1, count, body, 0)

        return (
            lambda: run(leaving, lambda c: c.start()),
            lambda: run(arriving, lambda c: c.wait_recv()),
            lambda: run(leaving, lambda c: c.wait_send()),
        )

    def across_wide(src, dst, send, recv):
        return over("wide", nw, wide, src, dst, send, recv)

    def across_narrow(src, dst, send, recv):
        return over("narrow", nn, narrow, src, dst, send, recv)

    lines = across_wide(lambda j: stage.at[j], lambda j: xr.at[j + 1], xs_s, xs_r)
    back = across_wide(
        lambda j: xsol.at[j, pl.ds(0, 6)], lambda j: xback.at[j, pl.ds(0, 6)], xb_s, xb_r
    )
    edges = across_narrow(lambda j: edge_s.at[j], lambda j: edge_r.at[j], yc_s, yc_r)
    datum = across_narrow(
        lambda j: dat_s.at[j, :, pl.ds(0, 6)], lambda j: dat_r.at[j, :, pl.ds(0, 6)], ys_s, ys_r
    )
    ends = across_narrow(
        lambda j: ends_s.at[j, :, pl.ds(0, 6)], lambda j: ends_r.at[j, :, pl.ds(0, 6)], yb_s, yb_r
    )

    pl.semaphore_wait(barrier, nw + nn - 2)

    halos = [
        pltpu.make_async_remote_copy(
            src_ref=src, dst_ref=dst, send_sem=hs.at[n], recv_sem=hr.at[n],
            device_id=peer, device_id_type=MESH,
        )
        for n, (src, dst, peer) in enumerate(
            (
                (sx_r, rx_l, {"wide": right}),
                (sx_l, rx_r, {"wide": left}),
                (sy_u, ry_d, {"narrow": upper}),
                (sy_d, ry_u, {"narrow": lower}),
            )
        )
    ]
    for copy in halos:
        copy.start()

    shape = (ROWS, pot.shape[2])
    lane = lax.broadcasted_iota(jnp.int32, shape, 1)
    sub = lax.broadcasted_iota(jnp.int32, shape, 0)
    length = pot.shape[2]

    def z_next(v):
        return jnp.where(lane == length - 1, 0.0, pltpu.roll(v, length - 1, 1))

    def z_prev(v):
        return jnp.where(lane == 0, 0.0, pltpu.roll(v, 1, 1))

    def y_next(v, edge):
        return jnp.where(sub == ROWS - 1, edge, pltpu.roll(v, ROWS - 1, 0))

    def y_prev(v, edge):
        return jnp.where(sub == 0, edge, pltpu.roll(v, 1, 0))

    tilt = (0.125, -0.125)
    div_z = []
    for x in range(2):
        p = pot[x]
        slope = z_next(p) - z_prev(p)
        row = []
        for k in range(2):
            q = act[k][x] * (vel[2, x] - tilt[k] * slope)
            row.append((z_next(q) - z_prev(q)) * 0.5)
        div_z.append(row)

    z_reduce(solid, z_inv, z_steps, length)
    for copy in halos:
        copy.wait()

    has_left = wide > 0
    has_right = wide < nw - 1
    has_down = narrow > 0
    has_up = narrow < nn - 1

    def kept(flag, v):
        return jnp.where(flag, v, 0.0)

    pots = [
        kept(has_left, rx_l[3]), kept(has_left, rx_l[4]), pot[0], pot[1],
        kept(has_right, rx_r[3]), kept(has_right, rx_r[4]),
    ]
    velx = [rx_l[2], vel[0, 0], vel[0, 1], rx_r[2]]
    for x in range(2):
        p = pot[x]
        down = kept(has_down, ry_d[x])
        up = kept(has_up, ry_u[x])
        slope_y = y_next(p, up[3:4]) - y_prev(p, down[4:5])
        slope_d = p[0:1] - down[3:4]
        slope_u = up[4:5] - p[7:8]
        for k in range(2):
            acts = [kept(has_left, rx_l[k]), act[k][0], act[k][1], kept(has_right, rx_r[k])]

            def flux_x(n):
                return acts[n] * (velx[n] - tilt[k] * (pots[n + 2] - pots[n]))

            div_x = (flux_x(x + 2) - flux_x(x)) * 0.5
            qy = act[k][x] * (vel[1, x] - tilt[k] * slope_y)
            q_down = down[k : k + 1] * (down[2:3] - tilt[k] * slope_d)
            q_up = up[k : k + 1] * (up[2:3] - tilt[k] * slope_u)
            div_y = (y_next(qy, q_up) - y_prev(qy, q_down)) * 0.5
            total = div_x + div_y + div_z[x][k]
            pack(2 * k + x, fl[x] * (conc[k, x] - 0.5 * total))
    to_stage(0)
    lines[0]()
    xr[pl.ds(wide + 1, 1)] = stage[pl.ds(wide, 1)]

    even, is_pot, rate = row_facts()

    def y_rows(y):
        return pl.ds(y * zt, zt)

    def y_mask(y):
        if 0 <= y < ROWS:
            m0, m1 = masks(stage[y_rows(y)])
        else:
            halo, flag = (ry_d, has_down) if y < 0 else (ry_u, has_up)

            def lanes(x):
                row = kept(flag, halo[x, 5:6])
                return jnp.stack([row[:, t * LANES : (t + 1) * LANES] for t in range(zt)])

            m0, m1 = lanes(0), lanes(1)
        return jnp.where(is_pot, 1.0, jnp.where(even, m0, m1))

    before, here = y_mask(-1), y_mask(0)
    c_prev = left_prev = None
    for y in range(ROWS):
        after = y_mask(y + 1)
        rm = rate * here
        lower = -rm * before
        upper = -rm * after
        if y == 0:
            lower = kept(has_down, lower)
        if y == ROWS - 1:
            upper = kept(has_up, upper)
        main = 1.0 + rm * (before + after)
        if y == 0:
            m = 1.0 / main
            left_now = -lower * m
        else:
            m = 1.0 / (main - lower * c_prev)
            left_now = -lower * left_prev * m
        y_m[y_rows(y)] = m
        y_am[y_rows(y)] = lower * m
        c_prev, left_prev = upper * m, left_now
        y_c[y_rows(y)] = c_prev
        y_left[y_rows(y)] = left_now
        before, here = here, after
    right_now = -c_prev
    y_right[y_rows(ROWS - 1)] = right_now
    edge_s[:, 2] = left_prev
    edge_s[:, 3] = right_now
    for y in range(ROWS - 2, -1, -1):
        c_now = y_c[y_rows(y)]
        left_prev = y_left[y_rows(y)] - c_now * left_prev
        right_now = -c_now * right_now
        y_left[y_rows(y)] = left_prev
        y_right[y_rows(y)] = right_now
    edge_s[:, 0] = left_prev
    edge_s[:, 1] = right_now
    edges[0]()
    edge_r[pl.ds(narrow, 1)] = edge_s[pl.ds(narrow, 1)]

    lines[1]()
    solve_tiles(xr, 1, (buf_a, buf_b), xsol, 0, nw, pad, True)
    back[0]()
    xback[pl.ds(wide, 1)] = xsol[pl.ds(wide, 1)]

    edges[1]()
    gain = jnp.zeros((ROWS, LANES), F32)
    for n in range(nn):
        first_left, first_right, last_left, last_right = (edge_r[n, i] for i in range(4))
        q = 1.0 / (1.0 - first_left * gain)
        ring[n, 0] = q
        ring[n, 1] = q * first_left
        ring[n, 2] = last_left * gain
        ring[n, 3] = q * first_right
        gain = last_right + last_left * gain * (q * first_right)
        ring[n, 4] = gain

    back[1]()
    d = xback[y_rows(0)] * y_m[y_rows(0)]
    y_sol[y_rows(0)] = d
    for y in range(1, ROWS):
        d = xback[y_rows(y)] * y_m[y_rows(y)] - y_am[y_rows(y)] * d
        y_sol[y_rows(y)] = d
    dat_s[:, 1] = d
    for y in range(ROWS - 2, -1, -1):
        d = y_sol[y_rows(y)] - y_c[y_rows(y)] * d
        y_sol[y_rows(y)] = d
    dat_s[:, 0] = d
    datum[0]()
    dat_r[pl.ds(narrow, 1)] = dat_s[pl.ds(narrow, 1)]
    datum[1]()
    firsts, lasts = [], []
    last = jnp.zeros((ROWS, LANES), F32)
    for n in range(nn):
        first = ring[n, 0] * dat_r[n, 0] + ring[n, 1] * last
        last = dat_r[n, 1] + edge_r[n, 2] * last + ring[n, 2] * first
        firsts.append(first)
        lasts.append(last)
    following = jnp.zeros((ROWS, LANES), F32)
    for n in range(nn - 1, -1, -1):
        ends_s[n, 1] = following
        following = firsts[n] + ring[n, 3] * following
        if n > 0:
            ends_s[n, 0] = lasts[n - 1] + ring[n - 1, 4] * following
        else:
            ends_s[n, 0] = jnp.zeros((ROWS, LANES), F32)
    ends[0]()
    ends_r[pl.ds(narrow, 1)] = ends_s[pl.ds(narrow, 1)]
    ends[1]()
    from_left, from_right = ends_r[:, 0], ends_r[:, 1]
    for y in range(ROWS):
        value = y_sol[y_rows(y)] + y_left[y_rows(y)] * from_left + y_right[y_rows(y)] * from_right
        for t in range(zt):
            packed[pl.ds(t * ROWS * ROWS + y, ROWS, stride=ROWS), :] = value[t]
    for k in range(3):
        for x, value in enumerate(z_solve(packed, k, z_inv, z_steps, length)):
            if k < 2:
                new_conc[k, x] = value
            else:
                new_pot[x] = value
    for exchange in (lines, back, edges, datum, ends):
        exchange[2]()

def hand_on(conc, pot, new_conc, new_pot):
    new_conc[...] = conc[...]
    new_pot[...] = pot[...]


def solution(mesh):
    nw, nn = mesh.shape["wide"], mesh.shape["narrow"]

    def shards(conc, potential, velocity, solid, fixed_charge):
        height = potential.shape[2]
        vmem = pl.BlockSpec(memory_space=pltpu.VMEM)
        tiles = (nw, ROWS, LANES)
        padded = (nw + 2, ROWS, LANES)
        plane = (5, ROWS, height)
        edge = (2, ROWS, height)
        bands = (3, 2 * nw, ROWS, LANES)
        dma = pltpu.SemaphoreType.DMA

        def body(*refs):
            main_kernel(nw, nn, *refs)

        results = pl.pallas_call(
            body,
            name="adi_step",
            out_shape=(
                jax.ShapeDtypeStruct(conc.shape, F32),
                jax.ShapeDtypeStruct(potential.shape, F32),
            ),
            in_specs=[pl.BlockSpec(memory_space=pl.ANY)] * 5,
            out_specs=(vmem, vmem),
            scratch_shapes=[
                pltpu.VMEM(conc.shape, F32),
                pltpu.VMEM(potential.shape, F32),
                pltpu.VMEM(velocity.shape, F32),
                pltpu.VMEM(solid.shape, jnp.int32),
                pltpu.VMEM(fixed_charge.shape, F32),
                dma((5,)),
            ]
            + [pltpu.VMEM(plane, F32)] * 4
            + [pltpu.VMEM(edge, F32)] * 4
            + [pltpu.VMEM((nw * ROWS, LANES), F32)]
            + [pltpu.VMEM(s, F32) for s in (tiles, padded, tiles, tiles, bands, bands)]
            + [pltpu.VMEM(tiles, F32)] * 6
            + [pltpu.VMEM((nn, n, ROWS, LANES), F32) for n in (4, 4, 2, 2, 2, 2, 5)]
            + [pltpu.VMEM((5, ROWS, height), F32)]
            + [pltpu.VMEM((5, (height - 1).bit_length(), 3, ROWS, height), F32)]
            + [dma((4,))] * 2
            + [dma((nw,))] * 4
            + [dma((nn,))] * 6,
            compiler_params=pltpu.CompilerParams(collective_id=0, has_side_effects=True),
        )(conc, potential, velocity, solid, fixed_charge)
        return pl.pallas_call(
            hand_on,
            name="hand_on",
            out_shape=tuple(jax.ShapeDtypeStruct(r.shape, F32) for r in results),
            in_specs=[vmem, vmem],
            out_specs=(vmem, vmem),
        )(*results)

    return jax.shard_map(
        shards,
        mesh=mesh,
        in_specs=(
            P(None, "wide", "narrow", None),
            P("wide", "narrow", None),
            P(None, "wide", "narrow", None),
            P("wide", "narrow", None),
            P("wide", "narrow", None),
        ),
        out_specs=(P(None, "wide", "narrow", None), P("wide", "narrow", None)),
        check_vma=False,
    )
```

```python
import jax
import jax.numpy as jnp
from jax import lax
from jax.experimental import pallas as pl
from jax.experimental.pallas import tpu as pltpu
from jax.sharding import PartitionSpec as P

F32 = jnp.float32
MESH = pl.DeviceIdType.MESH
LANES = 128
ROWS = 8
CHUNK = 8


def pcr(here, prev, succ):
    a, c, d = here
    ap, cp, dp = prev
    an, cn, dn = succ
    r = 1.0 / (1.0 - a * cp - c * an)
    return -(a * ap) * r, -(c * cn) * r, (d - a * dp - c * dn) * r


def row_facts():
    row = lax.broadcasted_iota(jnp.int32, (1, ROWS, LANES), 1)
    even = row % 2 == 0
    is_pot = row >= 4
    rate = jnp.where(row < 2, 8.0, jnp.where(row < 4, 5.0, jnp.where(row < 6, 16.0, 0.0)))
    return even, is_pot, rate.astype(F32)


def masks(tiles):
    return tiles[:, 6:7, :], tiles[:, 7:8, :]


def normal_bands(tiles, mask, mask_prev, mask_next, rate, is_first, is_last):
    rm = rate * mask
    inv = 1.0 / (1.0 + rm * (mask_prev + mask_next))
    lower = jnp.where(is_first, 0.0, -rm * mask_prev * inv)
    upper = jnp.where(is_last, 0.0, -rm * mask_next * inv)
    return lower, upper, tiles * inv


def solve_tiles(src_ref, src_pad, bufs, dst_ref, dst_pad, count, pad, paired):
    def build(i, _):
        even, is_pot, rate = row_facts()
        base = src_pad + i * CHUNK
        tiles = src_ref[pl.ds(base, CHUNK)]
        m0, m1 = masks(tiles)
        p0, p1 = masks(src_ref[pl.ds(base - 1, CHUNK)])
        n0, n1 = masks(src_ref[pl.ds(base + 1, CHUNK)])
        own = jnp.where(is_pot, 1.0, jnp.where(even, m0, m1))
        place = i * CHUNK + lax.broadcasted_iota(jnp.int32, (CHUNK, ROWS, LANES), 0)
        first = place == 0
        last = place == count - 1
        if paired:
            before = jnp.where(is_pot, 1.0, jnp.where(even, p1, m0))
            after = jnp.where(is_pot, 1.0, jnp.where(even, m1, n0))
            first = first & even
            last = last & jnp.logical_not(even)
        else:
            before = jnp.where(is_pot, 1.0, jnp.where(even, p0, p1))
            after = jnp.where(is_pot, 1.0, jnp.where(even, n0, n1))
        bands = normal_bands(tiles, own, before, after, rate, first, last)
        for k in range(3):
            bufs[0][k, pl.ds(pad + i * CHUNK, CHUNK)] = bands[k]
        return 0

    lax.fori_loop(0, count // CHUNK, build, 0)
    now = 0

    def window(buf, base):
        return tuple(buf[k, pl.ds(base, CHUNK)] for k in range(3))

    if paired:

        def pair_step(i, _):
            even, _, _ = row_facts()
            base = pad + i * CHUNK
            here = window(bufs[0], base)
            left = window(bufs[0], base - 1)
            right = window(bufs[0], base + 1)

            def up(v):
                return pltpu.roll(v, ROWS - 1, 1)

            def down(v):
                return pltpu.roll(v, 1, 1)

            prev = tuple(jnp.where(even, up(l), down(h)) for l, h in zip(left, here))
            succ = tuple(jnp.where(even, up(h), down(r)) for h, r in zip(here, right))
            for k, v in enumerate(pcr(here, prev, succ)):
                bufs[1][k, pl.ds(base, CHUNK)] = v
            return 0

        lax.fori_loop(0, count // CHUNK, pair_step, 0)
        now = 1

    spacing = 1
    while spacing < count:
        source, target = bufs[now], bufs[1 - now]
        final = spacing * 2 >= count

        def step(i, _, source=source, target=target, spacing=spacing, final=final):
            base = pad + i * CHUNK
            new = pcr(
                window(source, base), window(source, base - spacing), window(source, base + spacing)
            )
            if final:
                dst_ref[pl.ds(dst_pad + i * CHUNK, CHUNK)] = new[2]
            else:
                for k in range(3):
                    target[k, pl.ds(base, CHUNK)] = new[k]
            return 0

        lax.fori_loop(0, count // CHUNK, step, 0)
        now = 1 - now
        spacing *= 2


def z_reduce(solid, z_inv, z_steps, length):
    shape = (ROWS, length)
    lane = lax.broadcasted_iota(jnp.int32, shape, 1)
    for case in range(5):
        if case < 4:
            rm = (8.0, 5.0)[case // 2] * (1 - solid[case % 2]).astype(F32)
            mask = (1 - solid[case % 2]).astype(F32)
            before = jnp.where(lane == 0, 0.0, pltpu.roll(mask, 1, 1))
            after = jnp.where(lane == length - 1, 0.0, pltpu.roll(mask, length - 1, 1))
            inv = 1.0 / (1.0 + rm * (before + after))
            lower, upper = -rm * before * inv, -rm * after * inv
        else:
            inv = jnp.full(shape, 1.0 / 33.0, F32)
            lower = jnp.where(lane == 0, 0.0, -16.0 * inv)
            upper = jnp.where(lane == length - 1, 0.0, -16.0 * inv)
        z_inv[case] = inv
        spacing, step = 1, 0
        while spacing < length:
            lower_prev, upper_prev = (pltpu.roll(v, spacing, 1) for v in (lower, upper))
            lower_next, upper_next = (pltpu.roll(v, length - spacing, 1) for v in (lower, upper))
            r = 1.0 / (1.0 - lower * upper_prev - upper * lower_next)
            lower, upper = lower * r, upper * r
            for k, v in enumerate((r, lower, upper)):
                z_steps[case, step, k] = v
            lower, upper = -lower * lower_prev, -upper * upper_next
            spacing, step = spacing * 2, step + 1


def z_solve(packed, field, z_inv, z_steps, length):
    cases = [min(2 * field + x, 4) for x in range(2)]
    values = []
    for x in range(2):
        parts = [
            packed[pl.ds((t * ROWS + 2 * field + x) * ROWS, ROWS), :] for t in range(length // LANES)
        ]
        values.append(jnp.concatenate(parts, axis=1) * z_inv[cases[x]])
    spacing, step = 1, 0
    while spacing < length:
        for x in range(2):
            d = values[x]
            r, lower, upper = (z_steps[cases[x], step, k] for k in range(3))
            values[x] = (
                d * r - lower * pltpu.roll(d, spacing, 1) - upper * pltpu.roll(d, length - spacing, 1)
            )
        spacing, step = spacing * 2, step + 1
    return values


def main_kernel(
    nw, nn, conc_in, pot_in, vel_in, solid_in, fixed_in, new_conc, new_pot,
    conc, pot, vel, solid, fixed, in_sem,
    sx_r, sx_l, rx_l, rx_r, sy_u, sy_d, ry_d, ry_u, packed, stage, xr, xsol, xback,
    buf_a, buf_b, y_am, y_m, y_c, y_left, y_right, y_sol,
    edge_s, edge_r, dat_s, dat_r, ends_s, ends_r, ring, z_inv, z_steps,
    hs, hr, xs_s, xs_r, xb_s, xb_r, yc_s, yc_r, ys_s, ys_r, yb_s, yb_r,
):
    wide = lax.axis_index("wide")
    narrow = lax.axis_index("narrow")
    right = lax.rem(wide + 1, nw)
    left = lax.rem(wide + nw - 1, nw)
    upper = lax.rem(narrow + 1, nn)
    lower = lax.rem(narrow + nn - 1, nn)
    zt = pot.shape[2] // LANES
    pad = (buf_a.shape[1] - nw) // 2

    loads = [
        pltpu.make_async_copy(src, dst, in_sem.at[n])
        for n, (src, dst) in enumerate(
            (
                (solid_in, solid), (conc_in, conc), (pot_in, pot), (vel_in, vel), (fixed_in, fixed)
            )
        )
    ]
    for load in loads:
        load.start()
    barrier = pltpu.get_barrier_semaphore()

    def greet_wide(k, _):
        pl.semaphore_signal(
            barrier, inc=1, device_id={"wide": lax.rem(wide + nw // 2 + k, nw)}, device_id_type=MESH
        )
        return 0

    def greet_narrow(k, _):
        pl.semaphore_signal(
            barrier, inc=1, device_id={"narrow": lax.rem(narrow + k, nn)}, device_id_type=MESH
        )
        return 0

    lax.fori_loop(0, nw // 2, greet_wide, 0)
    lax.fori_loop(nw // 2 + 1, nw, greet_wide, 0)
    lax.fori_loop(1, nn, greet_narrow, 0)

    for load in loads:
        load.wait()
    fl = [(1 - solid[x]).astype(F32) for x in range(2)]
    act = [[fl[x] * conc[k, x] for x in range(2)] for k in range(2)]
    for k in range(2):
        sx_r[k] = act[k][1]
        sx_l[k] = act[k][0]
    sx_r[2] = vel[0, 1]
    sx_l[2] = vel[0, 0]
    for x in range(2):
        sx_r[3 + x] = pot[x]
        sx_l[3 + x] = pot[x]
        for k in range(2):
            sy_u[x, k : k + 1] = act[k][x][7:8]
            sy_d[x, k : k + 1] = act[k][x][0:1]
        sy_u[x, 2:3] = vel[1, x, 7:8]
        sy_d[x, 2:3] = vel[1, x, 0:1]
        sy_u[x, 3:5] = pot[x, 6:8]
        sy_d[x, 3:5] = pot[x, 0:2]
        sy_u[x, 5:6] = fl[x][7:8]
        sy_d[x, 5:6] = fl[x][0:1]
        sy_u[x, 6:8] = jnp.zeros((2, pot.shape[2]), F32)
        sy_d[x, 6:8] = jnp.zeros((2, pot.shape[2]), F32)
    nothing = jnp.zeros((pad, ROWS, LANES), F32)
    for buf in (buf_a, buf_b):
        for k in range(3):
            buf[k, pl.ds(0, pad)] = nothing
            buf[k, pl.ds(pad + nw, pad)] = nothing
    xr[pl.ds(0, 1)] = nothing[:1]
    xr[pl.ds(nw + 1, 1)] = nothing[:1]

    def pack(row, v):
        for t in range(zt):
            packed[pl.ds((t * ROWS + row) * ROWS, ROWS), :] = v[:, t * LANES : (t + 1) * LANES]

    def to_stage(first):
        for t in range(zt):
            for y in range(ROWS):
                rows = packed[pl.ds((t * ROWS + first) * ROWS + y, 4, stride=ROWS), :]
                stage[y * zt + t, first : first + 4] = rows

    for x in range(2):
        charge = act[0][x] - act[1][x] + (1.0 - fl[x]) * fixed[x]
        pack(4 + x, pot[x] + 2.0 * charge)
        pack(6 + x, fl[x])
    to_stage(4)

    def over(axis, count, me, src, dst, send, recv):
        def leaving(k):
            peer = lax.rem(me + k, count)
            return pltpu.make_async_remote_copy(
                src_ref=src(peer), dst_ref=dst(me), send_sem=send.at[peer], recv_sem=recv.at[me],
                device_id={axis: peer}, device_id_type=MESH,
            )

        def arriving(k):
            peer = lax.rem(me + k, count)
            return pltpu.make_async_remote_copy(
                src_ref=src(peer), dst_ref=dst(peer), send_sem=send.at[peer], recv_sem=recv.at[peer],
                device_id={axis: peer}, device_id_type=MESH,
            )

        def run(copy_of, act_on):
            def body(k, _):
                act_on(copy_of(k))
                return 0

            lax.fori_loop(1, count, body, 0)

        return (
            lambda: run(leaving, lambda c: c.start()),
            lambda: run(arriving, lambda c: c.wait_recv()),
            lambda: run(leaving, lambda c: c.wait_send()),
        )

    def across_wide(src, dst, send, recv):
        return over("wide", nw, wide, src, dst, send, recv)

    def across_narrow(src, dst, send, recv):
        return over("narrow", nn, narrow, src, dst, send, recv)

    lines = across_wide(lambda j: stage.at[j], lambda j: xr.at[j + 1], xs_s, xs_r)
    back = across_wide(
        lambda j: xsol.at[j, pl.ds(0, 6)], lambda j: xback.at[j, pl.ds(0, 6)], xb_s, xb_r
    )
    edges = across_narrow(lambda j: edge_s.at[j], lambda j: edge_r.at[j], yc_s, yc_r)
    datum = across_narrow(
        lambda j: dat_s.at[j, :, pl.ds(0, 6)], lambda j: dat_r.at[j, :, pl.ds(0, 6)], ys_s, ys_r
    )
    ends = across_narrow(
        lambda j: ends_s.at[j, :, pl.ds(0, 6)], lambda j: ends_r.at[j, :, pl.ds(0, 6)], yb_s, yb_r
    )

    pl.semaphore_wait(barrier, nw + nn - 2)

    halos = [
        pltpu.make_async_remote_copy(
            src_ref=src, dst_ref=dst, send_sem=hs.at[n], recv_sem=hr.at[n],
            device_id=peer, device_id_type=MESH,
        )
        for n, (src, dst, peer) in enumerate(
            (
                (sx_r, rx_l, {"wide": right}),
                (sx_l, rx_r, {"wide": left}),
                (sy_u, ry_d, {"narrow": upper}),
                (sy_d, ry_u, {"narrow": lower}),
            )
        )
    ]
    for copy in halos:
        copy.start()

    shape = (ROWS, pot.shape[2])
    lane = lax.broadcasted_iota(jnp.int32, shape, 1)
    sub = lax.broadcasted_iota(jnp.int32, shape, 0)
    length = pot.shape[2]

    def z_next(v):
        return jnp.where(lane == length - 1, 0.0, pltpu.roll(v, length - 1, 1))

    def z_prev(v):
        return jnp.where(lane == 0, 0.0, pltpu.roll(v, 1, 1))

    def y_next(v, edge):
        return jnp.where(sub == ROWS - 1, edge, pltpu.roll(v, ROWS - 1, 0))

    def y_prev(v, edge):
        return jnp.where(sub == 0, edge, pltpu.roll(v, 1, 0))

    tilt = (0.125, -0.125)
    div_z = []
    for x in range(2):
        p = pot[x]
        slope = z_next(p) - z_prev(p)
        row = []
        for k in range(2):
            q = act[k][x] * (vel[2, x] - tilt[k] * slope)
            row.append((z_next(q) - z_prev(q)) * 0.5)
        div_z.append(row)

    z_reduce(solid, z_inv, z_steps, length)
    for copy in halos:
        copy.wait()

    has_left = wide > 0
    has_right = wide < nw - 1
    has_down = narrow > 0
    has_up = narrow < nn - 1

    def kept(flag, v):
        return jnp.where(flag, v, 0.0)

    pots = [
        kept(has_left, rx_l[3]), kept(has_left, rx_l[4]), pot[0], pot[1],
        kept(has_right, rx_r[3]), kept(has_right, rx_r[4]),
    ]
    velx = [rx_l[2], vel[0, 0], vel[0, 1], rx_r[2]]
    for x in range(2):
        p = pot[x]
        down = kept(has_down, ry_d[x])
        up = kept(has_up, ry_u[x])
        slope_y = y_next(p, up[3:4]) - y_prev(p, down[4:5])
        slope_d = p[0:1] - down[3:4]
        slope_u = up[4:5] - p[7:8]
        for k in range(2):
            acts = [kept(has_left, rx_l[k]), act[k][0], act[k][1], kept(has_right, rx_r[k])]

            def flux_x(n):
                return acts[n] * (velx[n] - tilt[k] * (pots[n + 2] - pots[n]))

            div_x = (flux_x(x + 2) - flux_x(x)) * 0.5
            qy = act[k][x] * (vel[1, x] - tilt[k] * slope_y)
            q_down = down[k : k + 1] * (down[2:3] - tilt[k] * slope_d)
            q_up = up[k : k + 1] * (up[2:3] - tilt[k] * slope_u)
            div_y = (y_next(qy, q_up) - y_prev(qy, q_down)) * 0.5
            total = div_x + div_y + div_z[x][k]
            pack(2 * k + x, fl[x] * (conc[k, x] - 0.5 * total))
    to_stage(0)
    lines[0]()
    xr[pl.ds(wide + 1, 1)] = stage[pl.ds(wide, 1)]

    even, is_pot, rate = row_facts()

    def y_rows(y):
        return pl.ds(y * zt, zt)

    def y_mask(y):
        if 0 <= y < ROWS:
            m0, m1 = masks(stage[y_rows(y)])
        else:
            halo, flag = (ry_d, has_down) if y < 0 else (ry_u, has_up)

            def lanes(x):
                row = kept(flag, halo[x, 5:6])
                return jnp.stack([row[:, t * LANES : (t + 1) * LANES] for t in range(zt)])

            m0, m1 = lanes(0), lanes(1)
        return jnp.where(is_pot, 1.0, jnp.where(even, m0, m1))

    before, here = y_mask(-1), y_mask(0)
    c_prev = left_prev = None
    for y in range(ROWS):
        after = y_mask(y + 1)
        rm = rate * here
        lower = -rm * before
        upper = -rm * after
        if y == 0:
            lower = kept(has_down, lower)
        if y == ROWS - 1:
            upper = kept(has_up, upper)
        main = 1.0 + rm * (before + after)
        if y == 0:
            m = 1.0 / main
            left_now = -lower * m
        else:
            m = 1.0 / (main - lower * c_prev)
            left_now = -lower * left_prev * m
        y_m[y_rows(y)] = m
        y_am[y_rows(y)] = lower * m
        c_prev, left_prev = upper * m, left_now
        y_c[y_rows(y)] = c_prev
        y_left[y_rows(y)] = left_now
        before, here = here, after
    right_now = -c_prev
    y_right[y_rows(ROWS - 1)] = right_now
    edge_s[:, 2] = left_prev
    edge_s[:, 3] = right_now
    for y in range(ROWS - 2, -1, -1):
        c_now = y_c[y_rows(y)]
        left_prev = y_left[y_rows(y)] - c_now * left_prev
        right_now = -c_now * right_now
        y_left[y_rows(y)] = left_prev
        y_right[y_rows(y)] = right_now
    edge_s[:, 0] = left_prev
    edge_s[:, 1] = right_now
    edges[0]()
    edge_r[pl.ds(narrow, 1)] = edge_s[pl.ds(narrow, 1)]

    lines[1]()
    solve_tiles(xr, 1, (buf_a, buf_b), xsol, 0, nw, pad, True)
    back[0]()
    xback[pl.ds(wide, 1)] = xsol[pl.ds(wide, 1)]

    edges[1]()
    gain = jnp.zeros((ROWS, LANES), F32)
    for n in range(nn):
        first_left, first_right, last_left, last_right = (edge_r[n, i] for i in range(4))
        q = 1.0 / (1.0 - first_left * gain)
        ring[n, 0] = q
        ring[n, 1] = q * first_left
        ring[n, 2] = last_left * gain
        ring[n, 3] = q * first_right
        gain = last_right + last_left * gain * (q * first_right)
        ring[n, 4] = gain

    back[1]()
    d = xback[y_rows(0)] * y_m[y_rows(0)]
    y_sol[y_rows(0)] = d
    for y in range(1, ROWS):
        d = xback[y_rows(y)] * y_m[y_rows(y)] - y_am[y_rows(y)] * d
        y_sol[y_rows(y)] = d
    dat_s[:, 1] = d
    for y in range(ROWS - 2, -1, -1):
        d = y_sol[y_rows(y)] - y_c[y_rows(y)] * d
        y_sol[y_rows(y)] = d
    dat_s[:, 0] = d
    datum[0]()
    dat_r[pl.ds(narrow, 1)] = dat_s[pl.ds(narrow, 1)]
    datum[1]()
    firsts, lasts = [], []
    last = jnp.zeros((ROWS, LANES), F32)
    for n in range(nn):
        first = ring[n, 0] * dat_r[n, 0] + ring[n, 1] * last
        last = dat_r[n, 1] + edge_r[n, 2] * last + ring[n, 2] * first
        firsts.append(first)
        lasts.append(last)
    following = jnp.zeros((ROWS, LANES), F32)
    for n in range(nn - 1, -1, -1):
        ends_s[n, 1] = following
        following = firsts[n] + ring[n, 3] * following
        if n > 0:
            ends_s[n, 0] = lasts[n - 1] + ring[n - 1, 4] * following
        else:
            ends_s[n, 0] = jnp.zeros((ROWS, LANES), F32)
    ends[0]()
    ends_r[pl.ds(narrow, 1)] = ends_s[pl.ds(narrow, 1)]
    ends[1]()
    from_left, from_right = ends_r[:, 0], ends_r[:, 1]
    for y in range(ROWS):
        value = y_sol[y_rows(y)] + y_left[y_rows(y)] * from_left + y_right[y_rows(y)] * from_right
        for t in range(zt):
            packed[pl.ds(t * ROWS * ROWS + y, ROWS, stride=ROWS), :] = value[t]
    for k in range(3):
        for x, value in enumerate(z_solve(packed, k, z_inv, z_steps, length)):
            if k < 2:
                new_conc[k, x] = value
            else:
                new_pot[x] = value
    for exchange in (lines, back, edges, datum, ends):
        exchange[2]()

def hand_on(conc, pot, new_conc, new_pot):
    new_conc[...] = conc[...]
    new_pot[...] = pot[...]


def solution(mesh):
    nw, nn = mesh.shape["wide"], mesh.shape["narrow"]

    def shards(conc, potential, velocity, solid, fixed_charge):
        height = potential.shape[2]
        vmem = pl.BlockSpec(memory_space=pltpu.VMEM)
        tiles = (nw, ROWS, LANES)
        padded = (nw + 2, ROWS, LANES)
        plane = (5, ROWS, height)
        edge = (2, ROWS, height)
        bands = (3, 2 * nw, ROWS, LANES)
        dma = pltpu.SemaphoreType.DMA

        def body(*refs):
            main_kernel(nw, nn, *refs)

        results = pl.pallas_call(
            body,
            name="adi_step",
            out_shape=(pltpu.VMEM(conc.shape, F32), pltpu.VMEM(potential.shape, F32)),
            in_specs=[pl.BlockSpec(memory_space=pltpu.HBM)] * 5,
            out_specs=(vmem, vmem),
            scratch_shapes=[
                pltpu.VMEM(conc.shape, F32),
                pltpu.VMEM(potential.shape, F32),
                pltpu.VMEM(velocity.shape, F32),
                pltpu.VMEM(solid.shape, jnp.int32),
                pltpu.VMEM(fixed_charge.shape, F32),
                dma((5,)),
            ]
            + [pltpu.VMEM(plane, F32)] * 4
            + [pltpu.VMEM(edge, F32)] * 4
            + [pltpu.VMEM((nw * ROWS, LANES), F32)]
            + [pltpu.VMEM(s, F32) for s in (tiles, padded, tiles, tiles, bands, bands)]
            + [pltpu.VMEM(tiles, F32)] * 6
            + [pltpu.VMEM((nn, n, ROWS, LANES), F32) for n in (4, 4, 2, 2, 2, 2, 5)]
            + [pltpu.VMEM((5, ROWS, height), F32)]
            + [pltpu.VMEM((5, (height - 1).bit_length(), 3, ROWS, height), F32)]
            + [dma((4,))] * 2
            + [dma((nw,))] * 4
            + [dma((nn,))] * 6,
            compiler_params=pltpu.CompilerParams(
                collective_id=0, has_side_effects=True, vmem_limit_bytes=65000 * 1024
            ),
        )(conc, potential, velocity, solid, fixed_charge)
        return pl.pallas_call(
            hand_on,
            name="hand_on",
            compiler_params=pltpu.CompilerParams(vmem_limit_bytes=16 * 2**20),
            out_shape=tuple(jax.ShapeDtypeStruct(r.shape, F32) for r in results),
            in_specs=[vmem, vmem],
            out_specs=(vmem, vmem),
        )(*results)

    return jax.shard_map(
        shards,
        mesh=mesh,
        in_specs=(
            P(None, "wide", "narrow", None),
            P("wide", "narrow", None),
            P(None, "wide", "narrow", None),
            P("wide", "narrow", None),
            P("wide", "narrow", None),
        ),
        out_specs=(P(None, "wide", "narrow", None), P("wide", "narrow", None)),
        check_vma=False,
    )
```

```python
import jax
import jax.numpy as jnp
from jax import lax
from jax.experimental import pallas as pl
from jax.experimental.pallas import tpu as pltpu
from jax.sharding import PartitionSpec as P

F32 = jnp.float32
MESH = pl.DeviceIdType.MESH
LANES = 128
ROWS = 8
CHUNK = 8


def pcr(here, prev, succ):
    a, c, d = here
    ap, cp, dp = prev
    an, cn, dn = succ
    r = 1.0 / (1.0 - a * cp - c * an)
    return -(a * ap) * r, -(c * cn) * r, (d - a * dp - c * dn) * r


def row_facts():
    row = lax.broadcasted_iota(jnp.int32, (1, ROWS, LANES), 1)
    even = row % 2 == 0
    is_pot = row >= 4
    rate = jnp.where(row < 2, 8.0, jnp.where(row < 4, 5.0, jnp.where(row < 6, 16.0, 0.0)))
    return even, is_pot, rate.astype(F32)


def masks(tiles):
    return tiles[:, 6:7, :], tiles[:, 7:8, :]


def normal_bands(tiles, mask, mask_prev, mask_next, rate, is_first, is_last):
    rm = rate * mask
    inv = 1.0 / (1.0 + rm * (mask_prev + mask_next))
    lower = jnp.where(is_first, 0.0, -rm * mask_prev * inv)
    upper = jnp.where(is_last, 0.0, -rm * mask_next * inv)
    return lower, upper, tiles * inv


def solve_tiles(src_ref, src_pad, bufs, dst_ref, dst_pad, count, pad, paired):
    def build(i, _):
        even, is_pot, rate = row_facts()
        base = src_pad + i * CHUNK
        tiles = src_ref[pl.ds(base, CHUNK)]
        m0, m1 = masks(tiles)
        p0, p1 = masks(src_ref[pl.ds(base - 1, CHUNK)])
        n0, n1 = masks(src_ref[pl.ds(base + 1, CHUNK)])
        own = jnp.where(is_pot, 1.0, jnp.where(even, m0, m1))
        place = i * CHUNK + lax.broadcasted_iota(jnp.int32, (CHUNK, ROWS, LANES), 0)
        first = place == 0
        last = place == count - 1
        if paired:
            before = jnp.where(is_pot, 1.0, jnp.where(even, p1, m0))
            after = jnp.where(is_pot, 1.0, jnp.where(even, m1, n0))
            first = first & even
            last = last & jnp.logical_not(even)
        else:
            before = jnp.where(is_pot, 1.0, jnp.where(even, p0, p1))
            after = jnp.where(is_pot, 1.0, jnp.where(even, n0, n1))
        bands = normal_bands(tiles, own, before, after, rate, first, last)
        for k in range(3):
            bufs[0][k, pl.ds(pad + i * CHUNK, CHUNK)] = bands[k]
        return 0

    lax.fori_loop(0, count // CHUNK, build, 0)
    now = 0

    def window(buf, base):
        return tuple(buf[k, pl.ds(base, CHUNK)] for k in range(3))

    if paired:

        def pair_step(i, _):
            even, _, _ = row_facts()
            base = pad + i * CHUNK
            here = window(bufs[0], base)
            left = window(bufs[0], base - 1)
            right = window(bufs[0], base + 1)

            def up(v):
                return pltpu.roll(v, ROWS - 1, 1)

            def down(v):
                return pltpu.roll(v, 1, 1)

            prev = tuple(jnp.where(even, up(l), down(h)) for l, h in zip(left, here))
            succ = tuple(jnp.where(even, up(h), down(r)) for h, r in zip(here, right))
            for k, v in enumerate(pcr(here, prev, succ)):
                bufs[1][k, pl.ds(base, CHUNK)] = v
            return 0

        lax.fori_loop(0, count // CHUNK, pair_step, 0)
        now = 1

    spacing = 1
    while spacing < count:
        source, target = bufs[now], bufs[1 - now]
        final = spacing * 2 >= count

        def step(i, _, source=source, target=target, spacing=spacing, final=final):
            base = pad + i * CHUNK
            new = pcr(
                window(source, base), window(source, base - spacing), window(source, base + spacing)
            )
            if final:
                dst_ref[pl.ds(dst_pad + i * CHUNK, CHUNK)] = new[2]
            else:
                for k in range(3):
                    target[k, pl.ds(base, CHUNK)] = new[k]
            return 0

        lax.fori_loop(0, count // CHUNK, step, 0)
        now = 1 - now
        spacing *= 2


def z_reduce(solid, z_inv, z_steps, length):
    shape = (ROWS, length)
    lane = lax.broadcasted_iota(jnp.int32, shape, 1)
    for case in range(5):
        if case < 4:
            rm = (8.0, 5.0)[case // 2] * (1 - solid[case % 2]).astype(F32)
            mask = (1 - solid[case % 2]).astype(F32)
            before = jnp.where(lane == 0, 0.0, pltpu.roll(mask, 1, 1))
            after = jnp.where(lane == length - 1, 0.0, pltpu.roll(mask, length - 1, 1))
            inv = 1.0 / (1.0 + rm * (before + after))
            lower, upper = -rm * before * inv, -rm * after * inv
        else:
            inv = jnp.full(shape, 1.0 / 33.0, F32)
            lower = jnp.where(lane == 0, 0.0, -16.0 * inv)
            upper = jnp.where(lane == length - 1, 0.0, -16.0 * inv)
        z_inv[case] = inv
        spacing, step = 1, 0
        while spacing < length:
            lower_prev, upper_prev = (pltpu.roll(v, spacing, 1) for v in (lower, upper))
            lower_next, upper_next = (pltpu.roll(v, length - spacing, 1) for v in (lower, upper))
            r = 1.0 / (1.0 - lower * upper_prev - upper * lower_next)
            lower, upper = lower * r, upper * r
            for k, v in enumerate((r, lower, upper)):
                z_steps[case, step, k] = v
            lower, upper = -lower * lower_prev, -upper * upper_next
            spacing, step = spacing * 2, step + 1


def z_solve(packed, field, z_inv, z_steps, length):
    cases = [min(2 * field + x, 4) for x in range(2)]
    values = []
    for x in range(2):
        parts = [
            packed[pl.ds((t * ROWS + 2 * field + x) * ROWS, ROWS), :] for t in range(length // LANES)
        ]
        values.append(jnp.concatenate(parts, axis=1) * z_inv[cases[x]])
    spacing, step = 1, 0
    while spacing < length:
        for x in range(2):
            d = values[x]
            r, lower, upper = (z_steps[cases[x], step, k] for k in range(3))
            values[x] = (
                d * r - lower * pltpu.roll(d, spacing, 1) - upper * pltpu.roll(d, length - spacing, 1)
            )
        spacing, step = spacing * 2, step + 1
    return values


def main_kernel(
    nw, nn, conc_in, pot_in, vel_in, solid_in, fixed_in, new_conc, new_pot,
    conc, pot, vel, solid, fixed, in_sem,
    sx_r, sx_l, rx_l, rx_r, sy_u, sy_d, ry_d, ry_u, packed, stage, xr, xsol, xback,
    buf_a, buf_b, y_am, y_m, y_c, y_left, y_right, y_sol,
    edge_s, edge_r, dat_s, dat_r, ends_s, ends_r, ring, z_inv, z_steps,
    hs, hr, xs_s, xs_r, xb_s, xb_r, yc_s, yc_r, ys_s, ys_r, yb_s, yb_r,
):
    wide = lax.axis_index("wide")
    narrow = lax.axis_index("narrow")
    right = lax.rem(wide + 1, nw)
    left = lax.rem(wide + nw - 1, nw)
    upper = lax.rem(narrow + 1, nn)
    lower = lax.rem(narrow + nn - 1, nn)
    zt = pot.shape[2] // LANES
    pad = (buf_a.shape[1] - nw) // 2

    loads = [
        pltpu.make_async_copy(src, dst, in_sem.at[n])
        for n, (src, dst) in enumerate(
            (
                (solid_in, solid), (conc_in, conc), (pot_in, pot), (vel_in, vel), (fixed_in, fixed)
            )
        )
    ]
    for load in loads:
        load.start()
    barrier = pltpu.get_barrier_semaphore()

    def greet_wide(k, _):
        pl.semaphore_signal(
            barrier, inc=1, device_id={"wide": lax.rem(wide + nw // 2 + k, nw)}, device_id_type=MESH
        )
        return 0

    def greet_narrow(k, _):
        pl.semaphore_signal(
            barrier, inc=1, device_id={"narrow": lax.rem(narrow + k, nn)}, device_id_type=MESH
        )
        return 0

    lax.fori_loop(0, nw // 2, greet_wide, 0)
    lax.fori_loop(nw // 2 + 1, nw, greet_wide, 0)
    lax.fori_loop(1, nn, greet_narrow, 0)

    for load in loads:
        load.wait()
    fl = [(1 - solid[x]).astype(F32) for x in range(2)]
    act = [[fl[x] * conc[k, x] for x in range(2)] for k in range(2)]
    for k in range(2):
        sx_r[k] = act[k][1]
        sx_l[k] = act[k][0]
    sx_r[2] = vel[0, 1]
    sx_l[2] = vel[0, 0]
    for x in range(2):
        sx_r[3 + x] = pot[x]
        sx_l[3 + x] = pot[x]
        for k in range(2):
            sy_u[x, k : k + 1] = act[k][x][7:8]
            sy_d[x, k : k + 1] = act[k][x][0:1]
        sy_u[x, 2:3] = vel[1, x, 7:8]
        sy_d[x, 2:3] = vel[1, x, 0:1]
        sy_u[x, 3:5] = pot[x, 6:8]
        sy_d[x, 3:5] = pot[x, 0:2]
        sy_u[x, 5:6] = fl[x][7:8]
        sy_d[x, 5:6] = fl[x][0:1]
        sy_u[x, 6:8] = jnp.zeros((2, pot.shape[2]), F32)
        sy_d[x, 6:8] = jnp.zeros((2, pot.shape[2]), F32)
    def over(axis, count, me, src, dst, send, recv):
        def leaving(k):
            peer = lax.rem(me + k, count)
            return pltpu.make_async_remote_copy(
                src_ref=src(peer), dst_ref=dst(me), send_sem=send.at[peer], recv_sem=recv.at[me],
                device_id={axis: peer}, device_id_type=MESH,
            )

        def arriving(k):
            peer = lax.rem(me + k, count)
            return pltpu.make_async_remote_copy(
                src_ref=src(peer), dst_ref=dst(peer), send_sem=send.at[peer], recv_sem=recv.at[peer],
                device_id={axis: peer}, device_id_type=MESH,
            )

        def run(copy_of, act_on):
            def body(k, _):
                act_on(copy_of(k))
                return 0

            lax.fori_loop(1, count, body, 0)

        return (
            lambda: run(leaving, lambda c: c.start()),
            lambda: run(arriving, lambda c: c.wait_recv()),
            lambda: run(leaving, lambda c: c.wait_send()),
        )

    def across_wide(src, dst, send, recv):
        return over("wide", nw, wide, src, dst, send, recv)

    def across_narrow(src, dst, send, recv):
        return over("narrow", nn, narrow, src, dst, send, recv)

    lines = across_wide(lambda j: stage.at[j], lambda j: xr.at[j + 1], xs_s, xs_r)
    back = across_wide(
        lambda j: xsol.at[j, pl.ds(0, 6)], lambda j: xback.at[j, pl.ds(0, 6)], xb_s, xb_r
    )
    edges = across_narrow(lambda j: edge_s.at[j], lambda j: edge_r.at[j], yc_s, yc_r)
    datum = across_narrow(
        lambda j: dat_s.at[j, :, pl.ds(0, 6)], lambda j: dat_r.at[j, :, pl.ds(0, 6)], ys_s, ys_r
    )
    ends = across_narrow(
        lambda j: ends_s.at[j, :, pl.ds(0, 6)], lambda j: ends_r.at[j, :, pl.ds(0, 6)], yb_s, yb_r
    )

    pl.semaphore_wait(barrier, nw + nn - 2)

    halos = [
        pltpu.make_async_remote_copy(
            src_ref=src, dst_ref=dst, send_sem=hs.at[n], recv_sem=hr.at[n],
            device_id=peer, device_id_type=MESH,
        )
        for n, (src, dst, peer) in enumerate(
            (
                (sx_r, rx_l, {"wide": right}),
                (sx_l, rx_r, {"wide": left}),
                (sy_u, ry_d, {"narrow": upper}),
                (sy_d, ry_u, {"narrow": lower}),
            )
        )
    ]
    for copy in halos:
        copy.start()

    nothing = jnp.zeros((pad, ROWS, LANES), F32)
    for buf in (buf_a, buf_b):
        for k in range(3):
            buf[k, pl.ds(0, pad)] = nothing
            buf[k, pl.ds(pad + nw, pad)] = nothing
    xr[pl.ds(0, 1)] = nothing[:1]
    xr[pl.ds(nw + 1, 1)] = nothing[:1]

    def pack(row, v):
        for t in range(zt):
            packed[pl.ds((t * ROWS + row) * ROWS, ROWS), :] = v[:, t * LANES : (t + 1) * LANES]

    def to_stage(first):
        for t in range(zt):
            for y in range(ROWS):
                rows = packed[pl.ds((t * ROWS + first) * ROWS + y, 4, stride=ROWS), :]
                stage[y * zt + t, first : first + 4] = rows

    for x in range(2):
        charge = act[0][x] - act[1][x] + (1.0 - fl[x]) * fixed[x]
        pack(4 + x, pot[x] + 2.0 * charge)
        pack(6 + x, fl[x])
    to_stage(4)


    shape = (ROWS, pot.shape[2])
    lane = lax.broadcasted_iota(jnp.int32, shape, 1)
    sub = lax.broadcasted_iota(jnp.int32, shape, 0)
    length = pot.shape[2]

    def z_next(v):
        return jnp.where(lane == length - 1, 0.0, pltpu.roll(v, length - 1, 1))

    def z_prev(v):
        return jnp.where(lane == 0, 0.0, pltpu.roll(v, 1, 1))

    def y_next(v, edge):
        return jnp.where(sub == ROWS - 1, edge, pltpu.roll(v, ROWS - 1, 0))

    def y_prev(v, edge):
        return jnp.where(sub == 0, edge, pltpu.roll(v, 1, 0))

    tilt = (0.125, -0.125)
    div_z = []
    for x in range(2):
        p = pot[x]
        slope = z_next(p) - z_prev(p)
        row = []
        for k in range(2):
            q = act[k][x] * (vel[2, x] - tilt[k] * slope)
            row.append((z_next(q) - z_prev(q)) * 0.5)
        div_z.append(row)

    z_reduce(solid, z_inv, z_steps, length)
    for copy in halos:
        copy.wait()

    has_left = wide > 0
    has_right = wide < nw - 1
    has_down = narrow > 0
    has_up = narrow < nn - 1

    def kept(flag, v):
        return jnp.where(flag, v, 0.0)

    pots = [
        kept(has_left, rx_l[3]), kept(has_left, rx_l[4]), pot[0], pot[1],
        kept(has_right, rx_r[3]), kept(has_right, rx_r[4]),
    ]
    velx = [rx_l[2], vel[0, 0], vel[0, 1], rx_r[2]]
    for x in range(2):
        p = pot[x]
        down = kept(has_down, ry_d[x])
        up = kept(has_up, ry_u[x])
        slope_y = y_next(p, up[3:4]) - y_prev(p, down[4:5])
        slope_d = p[0:1] - down[3:4]
        slope_u = up[4:5] - p[7:8]
        for k in range(2):
            acts = [kept(has_left, rx_l[k]), act[k][0], act[k][1], kept(has_right, rx_r[k])]

            def flux_x(n):
                return acts[n] * (velx[n] - tilt[k] * (pots[n + 2] - pots[n]))

            div_x = (flux_x(x + 2) - flux_x(x)) * 0.5
            qy = act[k][x] * (vel[1, x] - tilt[k] * slope_y)
            q_down = down[k : k + 1] * (down[2:3] - tilt[k] * slope_d)
            q_up = up[k : k + 1] * (up[2:3] - tilt[k] * slope_u)
            div_y = (y_next(qy, q_up) - y_prev(qy, q_down)) * 0.5
            total = div_x + div_y + div_z[x][k]
            pack(2 * k + x, fl[x] * (conc[k, x] - 0.5 * total))
    to_stage(0)
    lines[0]()
    xr[pl.ds(wide + 1, 1)] = stage[pl.ds(wide, 1)]

    even, is_pot, rate = row_facts()

    def y_rows(y):
        return pl.ds(y * zt, zt)

    def y_mask(y):
        if 0 <= y < ROWS:
            m0, m1 = masks(stage[y_rows(y)])
        else:
            halo, flag = (ry_d, has_down) if y < 0 else (ry_u, has_up)

            def lanes(x):
                row = kept(flag, halo[x, 5:6])
                return jnp.stack([row[:, t * LANES : (t + 1) * LANES] for t in range(zt)])

            m0, m1 = lanes(0), lanes(1)
        return jnp.where(is_pot, 1.0, jnp.where(even, m0, m1))

    before, here = y_mask(-1), y_mask(0)
    c_prev = left_prev = None
    for y in range(ROWS):
        after = y_mask(y + 1)
        rm = rate * here
        lower = -rm * before
        upper = -rm * after
        if y == 0:
            lower = kept(has_down, lower)
        if y == ROWS - 1:
            upper = kept(has_up, upper)
        main = 1.0 + rm * (before + after)
        if y == 0:
            m = 1.0 / main
            left_now = -lower * m
        else:
            m = 1.0 / (main - lower * c_prev)
            left_now = -lower * left_prev * m
        y_m[y_rows(y)] = m
        y_am[y_rows(y)] = lower * m
        c_prev, left_prev = upper * m, left_now
        y_c[y_rows(y)] = c_prev
        y_left[y_rows(y)] = left_now
        before, here = here, after
    right_now = -c_prev
    y_right[y_rows(ROWS - 1)] = right_now
    edge_s[:, 2] = left_prev
    edge_s[:, 3] = right_now
    for y in range(ROWS - 2, -1, -1):
        c_now = y_c[y_rows(y)]
        left_prev = y_left[y_rows(y)] - c_now * left_prev
        right_now = -c_now * right_now
        y_left[y_rows(y)] = left_prev
        y_right[y_rows(y)] = right_now
    edge_s[:, 0] = left_prev
    edge_s[:, 1] = right_now
    edges[0]()
    edge_r[pl.ds(narrow, 1)] = edge_s[pl.ds(narrow, 1)]

    lines[1]()
    solve_tiles(xr, 1, (buf_a, buf_b), xsol, 0, nw, pad, True)
    back[0]()
    xback[pl.ds(wide, 1)] = xsol[pl.ds(wide, 1)]

    edges[1]()
    gain = jnp.zeros((ROWS, LANES), F32)
    for n in range(nn):
        first_left, first_right, last_left, last_right = (edge_r[n, i] for i in range(4))
        q = 1.0 / (1.0 - first_left * gain)
        ring[n, 0] = q
        ring[n, 1] = q * first_left
        ring[n, 2] = last_left * gain
        ring[n, 3] = q * first_right
        gain = last_right + last_left * gain * (q * first_right)
        ring[n, 4] = gain

    back[1]()
    d = xback[y_rows(0)] * y_m[y_rows(0)]
    y_sol[y_rows(0)] = d
    for y in range(1, ROWS):
        d = xback[y_rows(y)] * y_m[y_rows(y)] - y_am[y_rows(y)] * d
        y_sol[y_rows(y)] = d
    dat_s[:, 1] = d
    for y in range(ROWS - 2, -1, -1):
        d = y_sol[y_rows(y)] - y_c[y_rows(y)] * d
        y_sol[y_rows(y)] = d
    dat_s[:, 0] = d
    datum[0]()
    dat_r[pl.ds(narrow, 1)] = dat_s[pl.ds(narrow, 1)]
    datum[1]()
    firsts, lasts = [], []
    last = jnp.zeros((ROWS, LANES), F32)
    for n in range(nn):
        first = ring[n, 0] * dat_r[n, 0] + ring[n, 1] * last
        last = dat_r[n, 1] + edge_r[n, 2] * last + ring[n, 2] * first
        firsts.append(first)
        lasts.append(last)
    following = jnp.zeros((ROWS, LANES), F32)
    for n in range(nn - 1, -1, -1):
        ends_s[n, 1] = following
        following = firsts[n] + ring[n, 3] * following
        if n > 0:
            ends_s[n, 0] = lasts[n - 1] + ring[n - 1, 4] * following
        else:
            ends_s[n, 0] = jnp.zeros((ROWS, LANES), F32)
    ends[0]()
    ends_r[pl.ds(narrow, 1)] = ends_s[pl.ds(narrow, 1)]
    ends[1]()
    from_left, from_right = ends_r[:, 0], ends_r[:, 1]
    for y in range(ROWS):
        value = y_sol[y_rows(y)] + y_left[y_rows(y)] * from_left + y_right[y_rows(y)] * from_right
        for t in range(zt):
            packed[pl.ds(t * ROWS * ROWS + y, ROWS, stride=ROWS), :] = value[t]
    for k in range(3):
        for x, value in enumerate(z_solve(packed, k, z_inv, z_steps, length)):
            if k < 2:
                new_conc[k, x] = value
            else:
                new_pot[x] = value
    for exchange in (lines, back, edges, datum, ends):
        exchange[2]()

def hand_on(conc, pot, new_conc, new_pot):
    new_conc[...] = conc[...]
    new_pot[...] = pot[...]


def solution(mesh):
    nw, nn = mesh.shape["wide"], mesh.shape["narrow"]

    def shards(conc, potential, velocity, solid, fixed_charge):
        height = potential.shape[2]
        vmem = pl.BlockSpec(memory_space=pltpu.VMEM)
        tiles = (nw, ROWS, LANES)
        padded = (nw + 2, ROWS, LANES)
        plane = (5, ROWS, height)
        edge = (2, ROWS, height)
        bands = (3, 2 * nw, ROWS, LANES)
        dma = pltpu.SemaphoreType.DMA

        def body(*refs):
            main_kernel(nw, nn, *refs)

        results = pl.pallas_call(
            body,
            name="adi_step",
            out_shape=(pltpu.VMEM(conc.shape, F32), pltpu.VMEM(potential.shape, F32)),
            in_specs=[pl.BlockSpec(memory_space=pltpu.HBM)] * 5,
            out_specs=(vmem, vmem),
            scratch_shapes=[
                pltpu.VMEM(conc.shape, F32),
                pltpu.VMEM(potential.shape, F32),
                pltpu.VMEM(velocity.shape, F32),
                pltpu.VMEM(solid.shape, jnp.int32),
                pltpu.VMEM(fixed_charge.shape, F32),
                dma((5,)),
            ]
            + [pltpu.VMEM(plane, F32)] * 4
            + [pltpu.VMEM(edge, F32)] * 4
            + [pltpu.VMEM((nw * ROWS, LANES), F32)]
            + [pltpu.VMEM(s, F32) for s in (tiles, padded, tiles, tiles, bands, bands)]
            + [pltpu.VMEM(tiles, F32)] * 6
            + [pltpu.VMEM((nn, n, ROWS, LANES), F32) for n in (4, 4, 2, 2, 2, 2, 5)]
            + [pltpu.VMEM((5, ROWS, height), F32)]
            + [pltpu.VMEM((5, (height - 1).bit_length(), 3, ROWS, height), F32)]
            + [dma((4,))] * 2
            + [dma((nw,))] * 4
            + [dma((nn,))] * 6,
            compiler_params=pltpu.CompilerParams(
                collective_id=0, has_side_effects=True, vmem_limit_bytes=65000 * 1024
            ),
        )(conc, potential, velocity, solid, fixed_charge)
        return pl.pallas_call(
            hand_on,
            name="hand_on",
            compiler_params=pltpu.CompilerParams(vmem_limit_bytes=16 * 2**20),
            out_shape=tuple(jax.ShapeDtypeStruct(r.shape, F32) for r in results),
            in_specs=[vmem, vmem],
            out_specs=(vmem, vmem),
        )(*results)

    return jax.shard_map(
        shards,
        mesh=mesh,
        in_specs=(
            P(None, "wide", "narrow", None),
            P("wide", "narrow", None),
            P(None, "wide", "narrow", None),
            P("wide", "narrow", None),
            P("wide", "narrow", None),
        ),
        out_specs=(P(None, "wide", "narrow", None), P("wide", "narrow", None)),
        check_vma=False,
    )
```
